128 devices in a mesh: wide: 16 (over x, z), narrow: 8 (over y, core).
Axes of the slice: x: 4, y: 4, z: 4, core: 2. Of those that a mesh axis runs over, the one named last changes fastest.
Arguments:
- tensor_slab: float32 [512, 512, 2048], P(None, 'wide', 'narrow'), may hold values from -220 to 220
- start_basis: float32 [512, 64], replicated, may hold values from -6 to 6
Outputs:
- factor_basis: float32 [512, 64], replicated
- core_unfold: float32 [2048, 64, 512], P('narrow', 'wide')
The draws below stay inside these ranges and needn't reach their ends.
All inputs are finite; a program needn't handle non-finite values.
Results may differ from the reference program's by a relative error of at most 0.0003.
Values sent between devices are 32-bit elements; how exact they have to be, the bound alone decides.
A program may use at most 64 MiB of HBM per device.

```python
import jax
import jax.numpy as jnp
import numpy as np
from jax import lax

I1 = 512
RANK = 64
ITERS = 8
I2 = 512
I3 = 2048


def hadamard_rows(values):
    row_count = values.shape[0]
    half_width = 1
    while half_width < row_count:
        blocks = values.reshape(row_count // (2 * half_width), 2, half_width, -1)
        upper_half = blocks[:, 0]
        lower_half = blocks[:, 1]
        values = jnp.stack([upper_half + lower_half, upper_half - lower_half], axis=1).reshape(row_count, -1)
        half_width = half_width * 2
    return values


def draw_tensor_slab(key, part):
    key_base = jax.random.fold_in(key, 11)
    key_rows = jax.random.fold_in(key, 12)
    key_fiber = jax.random.fold_in(key, 13)
    key_second = jax.random.fold_in(key, 14)
    decay_rate = 0.993
    first_levels = jax.random.randint(key_base, (I1, I2 * I3), -48, 49)
    second_levels = jax.random.randint(key_second, (I1, I2 * I3), -48, 49)
    levels = (first_levels + second_levels).astype(jnp.float32)
    amplitude = jnp.asarray(np.floor(64.0 * decay_rate ** np.arange(I1) + 0.5), jnp.float32)
    mixed_rows = hadamard_rows(levels * amplitude[:, None]) / 16384.0
    base_field = jnp.clip(mixed_rows, -4.0, 4.0).reshape(I1, I2, I3)
    row_scale = jnp.exp(jax.random.uniform(key_rows, (I1, 1, 1), jnp.float32, -1.2, 1.1))
    fiber_scale = jnp.exp(jax.random.uniform(key_fiber, (1, I2, I3), jnp.float32, -0.69, 0.69))
    ramp_second = 1.0 + 2.0 * jnp.arange(I2, dtype=jnp.float32) / max(I2 - 1, 1)
    ramp_third = 1.0 + 2.0 * jnp.arange(I3, dtype=jnp.float32) / max(I3 - 1, 1)
    return base_field * row_scale * fiber_scale * ramp_second[None, :, None] * ramp_third[None, None, :]


def normal_values(stream_key, dims, scale, bound, kind=jnp.bfloat16):
    entries = scale * jax.random.normal(stream_key, dims, jnp.float32)
    return jnp.clip(entries, min=-bound, max=bound).astype(kind)


def setup_inputs(seed: int = 0) -> dict:
    keys = jax.random.split(jax.random.key(seed), 3)
    return {
        "tensor_slab": draw_tensor_slab(jax.random.fold_in(keys[2], 71), 0),
        "start_basis": normal_values(keys[1], (I1, RANK), 1.0, 6.0, jnp.float32),
    }


def orthonormal(block, inner):
    lower_factor = jnp.linalg.cholesky(inner)
    return jax.scipy.linalg.solve_triangular(lower_factor, block.T, lower=True).T

def reference(tensor_slab, start_basis):
    highest = lax.Precision.HIGHEST
    unfold = tensor_slab.reshape(I1, -1)
    gram = jnp.dot(unfold.astype(jnp.float32), unfold.T.astype(jnp.float32), precision=highest, preferred_element_type=jnp.float32)
    basis = start_basis
    for sweep_index in range(ITERS):
        block = jnp.dot(gram, basis, precision=highest)
        basis = orthonormal(block, jnp.dot(block.T, block, precision=highest))
    core_unfold = jnp.einsum('ir,ijl->lrj', basis, tensor_slab, precision=highest)
    return (basis, core_unfold)
```

```python
import jax
import jax.numpy as jnp
from jax import lax
from jax.sharding import PartitionSpec as P

I1 = 512
ITERS = 8


def orthonormal(block, inner):
    lower_factor = jnp.linalg.cholesky(inner)
    return jax.scipy.linalg.solve_triangular(lower_factor, block.T, lower=True).T


def shards(tensor_slab, start_basis):
    highest = lax.Precision.HIGHEST
    high = lax.Precision.HIGH
    _, cols, depth = tensor_slab.shape
    unfold = tensor_slab.reshape(I1, -1)
    basis = start_basis
    local_gram = jnp.dot(unfold, unfold.T, precision=high, preferred_element_type=jnp.float32)
    gram_full = lax.psum(local_gram, ("wide", "narrow"))
    for sweep_index in range(ITERS):
        block = jnp.dot(gram_full, basis, precision=highest)
        basis = orthonormal(block, jnp.dot(block.T, block, precision=highest))
    proj = jnp.einsum("ir,ijl->rjl", basis, tensor_slab, precision=high, preferred_element_type=jnp.float32)
    proj = lax.all_to_all(proj, "wide", split_axis=0, concat_axis=1, tiled=True)
    core_unfold = jnp.transpose(proj, (2, 0, 1))
    return (basis, core_unfold)


def solution(mesh):
    placed = (P(None, "wide", "narrow"), P())
    return jax.shard_map(
        shards,
        mesh=mesh,
        in_specs=placed,
        out_specs=(P(), P("narrow", "wide", None)),
        check_vma=False,
    )
```

```python
import functools

import jax
import jax.numpy as jnp
from jax import lax
from jax.experimental import pallas as pl
from jax.experimental.pallas import tpu as pltpu
from jax.sharding import PartitionSpec as P

I1 = 512
ITERS = 8
MESH = pl.DeviceIdType.MESH


def orthonormal(block, inner):
    lower_factor = jnp.linalg.cholesky(inner)
    return jax.scipy.linalg.solve_triangular(lower_factor, block.T, lower=True).T


def _allreduce_kernel(x_ref, o_ref, acc1, acc2, acc3, acc4, r1, r2, r3, r4, full, send_sems, recv_sems):
    w = lax.axis_index("wide")
    n = lax.axis_index("narrow")
    px, pz = w // 4, w % 4
    py, pc = n // 2, n % 2
    rows, cols = x_ref.shape
    h1 = rows // 2
    h2 = h1 // 4
    h3 = h2 // 4
    cw = cols // 4

    core_dev = (w, py * 2 + (1 - pc))

    def y_dev(o):
        return (w, ((py + o) % 4) * 2 + pc)

    def x_dev(o):
        return (((px + o) % 4) * 4 + pz, n)

    def z_dev(o):
        return (px * 4 + (pz + o) % 4, n)

    partners = [core_dev] + [y_dev(o) for o in (1, 2, 3)] + [x_dev(o) for o in (1, 2, 3)] + [z_dev(o) for o in (1, 2, 3)]
    barrier = pltpu.get_barrier_semaphore()
    for dev in partners:
        pl.semaphore_signal(barrier, inc=1, device_id=dev, device_id_type=MESH)
    pl.semaphore_wait(barrier, len(partners))

    slot = [0]

    def send(src, dst, dev):
        k = slot[0]
        slot[0] += 1
        cp = pltpu.make_async_remote_copy(
            src_ref=src, dst_ref=dst, send_sem=send_sems.at[k], recv_sem=recv_sems.at[k],
            device_id=dev, device_id_type=MESH)
        cp.start()
        return cp

    def wait_all(cps):
        for cp in cps:
            cp.wait()

    cp = send(x_ref.at[pl.ds(pl.multiple_of((1 - pc) * h1, 8), h1)], r1, core_dev)
    cp.wait()
    acc1[...] = x_ref[pl.ds(pl.multiple_of(pc * h1, 8), h1), :] + r1[...]

    cps = []
    for o in (1, 2, 3):
        q = (py + o) % 4
        cps.append(send(acc1.at[pl.ds(pl.multiple_of(q * h2, 8), h2)], r2.at[o - 1], y_dev(o)))
    wait_all(cps)
    acc2[...] = acc1[pl.ds(pl.multiple_of(py * h2, 8), h2), :] + r2[0] + r2[1] + r2[2]

    cps = []
    for o in (1, 2, 3):
        q = (px + o) % 4
        cps.append(send(acc2.at[pl.ds(pl.multiple_of(q * h3, 8), h3)], r3.at[o - 1], x_dev(o)))
    wait_all(cps)
    acc3[...] = acc2[pl.ds(pl.multiple_of(px * h3, 8), h3), :] + r3[0] + r3[1] + r3[2]

    cps = []
    for o in (1, 2, 3):
        q = (pz + o) % 4
        cps.append(send(acc3.at[:, pl.ds(pl.multiple_of(q * cw, 128), cw)], r4.at[o - 1], z_dev(o)))
    wait_all(cps)
    acc4[...] = acc3[:, pl.ds(pl.multiple_of(pz * cw, 128), cw)] + r4[0] + r4[1] + r4[2]

    row1 = pc * h1
    row2 = row1 + py * h2
    row3 = row2 + px * h3
    full[pl.ds(pl.multiple_of(row3, 8), h3), pl.ds(pl.multiple_of(pz * cw, 128), cw)] = acc4[...]

    mine = full.at[pl.ds(pl.multiple_of(row3, 8), h3), pl.ds(pl.multiple_of(pz * cw, 128), cw)]
    wait_all([send(mine, mine, z_dev(o)) for o in (1, 2, 3)])
    mine = full.at[pl.ds(pl.multiple_of(row3, 8), h3)]
    wait_all([send(mine, mine, x_dev(o)) for o in (1, 2, 3)])
    mine = full.at[pl.ds(pl.multiple_of(row2, 8), h2)]
    wait_all([send(mine, mine, y_dev(o)) for o in (1, 2, 3)])
    mine = full.at[pl.ds(pl.multiple_of(row1, 8), h1)]
    send(mine, mine, core_dev).wait()

    o_ref[...] = full[...]


def allreduce_all(x):
    rows, cols = x.shape
    h1 = rows // 2
    h2 = h1 // 4
    h3 = h2 // 4
    cw = cols // 4
    f32 = jnp.float32
    return pl.pallas_call(
        _allreduce_kernel,
        out_shape=jax.ShapeDtypeStruct((rows, cols), f32),
        in_specs=[pl.BlockSpec(memory_space=pltpu.VMEM)],
        out_specs=pl.BlockSpec(memory_space=pltpu.VMEM),
        scratch_shapes=[
            pltpu.VMEM((h1, cols), f32),
            pltpu.VMEM((h2, cols), f32),
            pltpu.VMEM((h3, cols), f32),
            pltpu.VMEM((h3, cw), f32),
            pltpu.VMEM((h1, cols), f32),
            pltpu.VMEM((3, h2, cols), f32),
            pltpu.VMEM((3, h3, cols), f32),
            pltpu.VMEM((3, h3, cw), f32),
            pltpu.VMEM((rows, cols), f32),
            pltpu.SemaphoreType.DMA((20,)),
            pltpu.SemaphoreType.DMA((20,)),
        ],
        compiler_params=pltpu.CompilerParams(collective_id=0, has_side_effects=True),
    )(x)


def shards(tensor_slab, start_basis):
    highest = lax.Precision.HIGHEST
    high = lax.Precision.HIGH
    unfold = tensor_slab.reshape(I1, -1)
    basis = start_basis
    local_gram = jnp.dot(unfold, unfold.T, precision=high, preferred_element_type=jnp.float32)
    gram_full = allreduce_all(local_gram)
    for sweep_index in range(ITERS):
        block = jnp.dot(gram_full, basis, precision=highest)
        basis = orthonormal(block, jnp.dot(block.T, block, precision=highest))
    proj = jnp.einsum("ir,ijl->rjl", basis, tensor_slab, precision=high, preferred_element_type=jnp.float32)
    proj = lax.all_to_all(proj, "wide", split_axis=0, concat_axis=1, tiled=True)
    core_unfold = jnp.transpose(proj, (2, 0, 1))
    return (basis, core_unfold)


def solution(mesh):
    placed = (P(None, "wide", "narrow"), P())
    return jax.shard_map(
        shards,
        mesh=mesh,
        in_specs=placed,
        out_specs=(P(), P("narrow", "wide", None)),
        check_vma=False,
    )
```

```python
import functools

import jax
import jax.numpy as jnp
from jax import lax
from jax.experimental import pallas as pl
from jax.experimental.pallas import tpu as pltpu
from jax.sharding import PartitionSpec as P

I1 = 512
ITERS = 8
MESH = pl.DeviceIdType.MESH


def orthonormal(block, inner):
    lower_factor = jnp.linalg.cholesky(inner)
    return jax.scipy.linalg.solve_triangular(lower_factor, block.T, lower=True).T


def _allreduce_kernel(x_ref, o_ref, acc1, acc2, acc3, acc4, r1, r2, r3, r4, full, send_sems, recv_sems):
    w = lax.axis_index("wide")
    n = lax.axis_index("narrow")
    px, pz = w // 4, w % 4
    py, pc = n // 2, n % 2
    rows, cols = x_ref.shape
    h1 = rows // 2
    h2 = h1 // 4
    h3 = h2 // 4
    cw = cols // 4

    core_dev = (w, py * 2 + (1 - pc))

    def y_dev(o):
        return (w, ((py + o) % 4) * 2 + pc)

    def x_dev(o):
        return (((px + o) % 4) * 4 + pz, n)

    def z_dev(o):
        return (px * 4 + (pz + o) % 4, n)

    partners = [core_dev] + [y_dev(o) for o in (1, 2, 3)] + [x_dev(o) for o in (1, 2, 3)] + [z_dev(o) for o in (1, 2, 3)]
    barrier = pltpu.get_barrier_semaphore()
    for dev in partners:
        pl.semaphore_signal(barrier, inc=1, device_id=dev, device_id_type=MESH)
    pl.semaphore_wait(barrier, len(partners))

    slot = [0]

    def send(src, dst, dev):
        k = slot[0]
        slot[0] += 1
        cp = pltpu.make_async_remote_copy(
            src_ref=src, dst_ref=dst, send_sem=send_sems.at[k], recv_sem=recv_sems.at[k],
            device_id=dev, device_id_type=MESH)
        cp.start()
        return cp

    def wait_all(cps):
        for cp in cps:
            cp.wait()

    cp = send(x_ref.at[pl.ds(pl.multiple_of((1 - pc) * h1, 8), h1)], r1, core_dev)
    cp.wait()
    acc1[...] = x_ref[pl.ds(pl.multiple_of(pc * h1, 8), h1), :] + r1[...]

    cps = []
    for o in (1, 2, 3):
        q = (py + o) % 4
        cps.append(send(acc1.at[pl.ds(pl.multiple_of(q * h2, 8), h2)], r2.at[o - 1], y_dev(o)))
    wait_all(cps)
    acc2[...] = acc1[pl.ds(pl.multiple_of(py * h2, 8), h2), :] + r2[0] + r2[1] + r2[2]

    cps = []
    for o in (1, 2, 3):
        q = (px + o) % 4
        cps.append(send(acc2.at[pl.ds(pl.multiple_of(q * h3, 8), h3)], r3.at[o - 1], x_dev(o)))
    wait_all(cps)
    acc3[...] = acc2[pl.ds(pl.multiple_of(px * h3, 8), h3), :] + r3[0] + r3[1] + r3[2]

    cps = []
    for o in (1, 2, 3):
        q = (pz + o) % 4
        cps.append(send(acc3.at[:, pl.ds(pl.multiple_of(q * cw, 128), cw)], r4.at[o - 1], z_dev(o)))
    wait_all(cps)
    acc4[...] = acc3[:, pl.ds(pl.multiple_of(pz * cw, 128), cw)] + r4[0] + r4[1] + r4[2]

    row1 = pc * h1
    row2 = row1 + py * h2
    row3 = row2 + px * h3
    full[pl.ds(pl.multiple_of(row3, 8), h3), pl.ds(pl.multiple_of(pz * cw, 128), cw)] = acc4[...]

    mine = full.at[pl.ds(pl.multiple_of(row3, 8), h3), pl.ds(pl.multiple_of(pz * cw, 128), cw)]
    wait_all([send(mine, mine, z_dev(o)) for o in (1, 2, 3)])
    mine = full.at[pl.ds(pl.multiple_of(row3, 8), h3)]
    wait_all([send(mine, mine, x_dev(o)) for o in (1, 2, 3)])
    mine = full.at[pl.ds(pl.multiple_of(row2, 8), h2)]
    wait_all([send(mine, mine, y_dev(o)) for o in (1, 2, 3)])
    mine = full.at[pl.ds(pl.multiple_of(row1, 8), h1)]
    send(mine, mine, core_dev).wait()

    o_ref[...] = full[...]


def allreduce_all(x):
    rows, cols = x.shape
    h1 = rows // 2
    h2 = h1 // 4
    h3 = h2 // 4
    cw = cols // 4
    f32 = jnp.float32
    return pl.pallas_call(
        _allreduce_kernel,
        out_shape=jax.ShapeDtypeStruct((rows, cols), f32),
        in_specs=[pl.BlockSpec(memory_space=pltpu.VMEM)],
        out_specs=pl.BlockSpec(memory_space=pltpu.VMEM),
        scratch_shapes=[
            pltpu.VMEM((h1, cols), f32),
            pltpu.VMEM((h2, cols), f32),
            pltpu.VMEM((h3, cols), f32),
            pltpu.VMEM((h3, cw), f32),
            pltpu.VMEM((h1, cols), f32),
            pltpu.VMEM((3, h2, cols), f32),
            pltpu.VMEM((3, h3, cols), f32),
            pltpu.VMEM((3, h3, cw), f32),
            pltpu.VMEM((rows, cols), f32),
            pltpu.SemaphoreType.DMA((20,)),
            pltpu.SemaphoreType.DMA((20,)),
        ],
        compiler_params=pltpu.CompilerParams(collective_id=0, has_side_effects=True),
    )(x)


def _subspace_kernel(g_ref, b0_ref, o_ref):
    highest = lax.Precision.HIGHEST
    rank = b0_ref.shape[0]
    rows = lax.broadcasted_iota(jnp.int32, (rank, rank), 0)
    cols = lax.broadcasted_iota(jnp.int32, (rank, rank), 1)
    col_idx = lax.broadcasted_iota(jnp.int32, (rank, 1), 0)
    row_idx = lax.broadcasted_iota(jnp.int32, (1, rank), 1)
    eye = jnp.where(rows == cols, 1.0, 0.0).astype(jnp.float32)
    zero = jnp.zeros((rank, rank), jnp.float32)

    def step(j, carry):
        m, e, z = carry
        at_row = rows == j
        row_m = jnp.sum(jnp.where(at_row, m, 0.0), axis=0, keepdims=True)
        col_m = jnp.sum(jnp.where(cols == j, m, 0.0), axis=1, keepdims=True)
        d = jnp.sum(jnp.where(row_idx == j, row_m, 0.0), axis=1, keepdims=True)
        s = lax.rsqrt(d)
        c = jnp.where(col_idx >= j, col_m * s, 0.0)
        r = jnp.where(row_idx >= j, row_m * s, 0.0)
        m = m - c * r
        zr = jnp.sum(jnp.where(at_row, e, 0.0), axis=0, keepdims=True) * s
        e = e - c * zr
        z = jnp.where(at_row, zr, z)
        return m, e, z

    def sweep(_, basis_t):
        block_t = jnp.dot(basis_t, g_ref[...], precision=highest, preferred_element_type=jnp.float32)
        inner = lax.dot_general(block_t, block_t, (((1,), (1,)), ((), ())), precision=highest,
                                preferred_element_type=jnp.float32)
        _, _, l_inv = lax.fori_loop(0, rank, step, (inner, eye, zero))
        return jnp.dot(l_inv, block_t, precision=highest, preferred_element_type=jnp.float32)

    o_ref[...] = lax.fori_loop(0, ITERS, sweep, b0_ref[...])


def subspace_iterate(gram, start_basis):
    basis_t = pl.pallas_call(
        _subspace_kernel,
        out_shape=jax.ShapeDtypeStruct(start_basis.shape[::-1], jnp.float32),
        in_specs=[pl.BlockSpec(memory_space=pltpu.VMEM)] * 2,
        out_specs=pl.BlockSpec(memory_space=pltpu.VMEM),
    )(gram, start_basis.T)
    return basis_t.T


def shards(tensor_slab, start_basis):
    highest = lax.Precision.HIGHEST
    high = lax.Precision.HIGH
    unfold = tensor_slab.reshape(I1, -1)
    basis = start_basis
    local_gram = jnp.dot(unfold, unfold.T, precision=high, preferred_element_type=jnp.float32)
    gram_full = allreduce_all(local_gram)
    basis = subspace_iterate(gram_full, start_basis)
    proj = jnp.einsum("ir,ijl->rjl", basis, tensor_slab, precision=high, preferred_element_type=jnp.float32)
    proj = lax.all_to_all(proj, "wide", split_axis=0, concat_axis=1, tiled=True)
    core_unfold = jnp.transpose(proj, (2, 0, 1))
    return (basis, core_unfold)


def solution(mesh):
    placed = (P(None, "wide", "narrow"), P())
    return jax.shard_map(
        shards,
        mesh=mesh,
        in_specs=placed,
        out_specs=(P(), P("narrow", "wide", None)),
        check_vma=False,
    )
```

```python
import functools

import jax
import jax.numpy as jnp
from jax import lax
from jax.experimental import pallas as pl
from jax.experimental.pallas import tpu as pltpu
from jax.sharding import PartitionSpec as P

I1 = 512
ITERS = 8
MESH = pl.DeviceIdType.MESH


def orthonormal(block, inner):
    lower_factor = jnp.linalg.cholesky(inner)
    return jax.scipy.linalg.solve_triangular(lower_factor, block.T, lower=True).T


def _allreduce_kernel(x_ref, o_ref, acc1, acc2, acc3, acc4, r1, r2, r3, r4, full, send_sems, recv_sems):
    w = lax.axis_index("wide")
    n = lax.axis_index("narrow")
    px, pz = w // 4, w % 4
    py, pc = n // 2, n % 2
    rows, cols = x_ref.shape
    h1 = rows // 2
    h2 = h1 // 4
    h3 = h2 // 4
    cw = cols // 4

    core_dev = (w, py * 2 + (1 - pc))

    def y_dev(o):
        return (w, ((py + o) % 4) * 2 + pc)

    def x_dev(o):
        return (((px + o) % 4) * 4 + pz, n)

    def z_dev(o):
        return (px * 4 + (pz + o) % 4, n)

    partners = [core_dev] + [y_dev(o) for o in (1, 2, 3)] + [x_dev(o) for o in (1, 2, 3)] + [z_dev(o) for o in (1, 2, 3)]
    barrier = pltpu.get_barrier_semaphore()
    for dev in partners:
        pl.semaphore_signal(barrier, inc=1, device_id=dev, device_id_type=MESH)
    pl.semaphore_wait(barrier, len(partners))

    slot = [0]

    def send(src, dst, dev):
        k = slot[0]
        slot[0] += 1
        cp = pltpu.make_async_remote_copy(
            src_ref=src, dst_ref=dst, send_sem=send_sems.at[k], recv_sem=recv_sems.at[k],
            device_id=dev, device_id_type=MESH)
        cp.start()
        return cp

    def wait_all(cps):
        for cp in cps:
            cp.wait()

    cp = send(x_ref.at[pl.ds(pl.multiple_of((1 - pc) * h1, 8), h1)], r1, core_dev)
    cp.wait()
    acc1[...] = x_ref[pl.ds(pl.multiple_of(pc * h1, 8), h1), :] + r1[...]

    cps = []
    for o in (1, 2, 3):
        q = (py + o) % 4
        cps.append(send(acc1.at[pl.ds(pl.multiple_of(q * h2, 8), h2)], r2.at[o - 1], y_dev(o)))
    wait_all(cps)
    acc2[...] = acc1[pl.ds(pl.multiple_of(py * h2, 8), h2), :] + r2[0] + r2[1] + r2[2]

    cps = []
    for o in (1, 2, 3):
        q = (px + o) % 4
        cps.append(send(acc2.at[pl.ds(pl.multiple_of(q * h3, 8), h3)], r3.at[o - 1], x_dev(o)))
    wait_all(cps)
    acc3[...] = acc2[pl.ds(pl.multiple_of(px * h3, 8), h3), :] + r3[0] + r3[1] + r3[2]

    cps = []
    for o in (1, 2, 3):
        q = (pz + o) % 4
        cps.append(send(acc3.at[:, pl.ds(pl.multiple_of(q * cw, 128), cw)], r4.at[o - 1], z_dev(o)))
    wait_all(cps)
    acc4[...] = acc3[:, pl.ds(pl.multiple_of(pz * cw, 128), cw)] + r4[0] + r4[1] + r4[2]

    row1 = pc * h1
    row2 = row1 + py * h2
    row3 = row2 + px * h3
    full[pl.ds(pl.multiple_of(row3, 8), h3), pl.ds(pl.multiple_of(pz * cw, 128), cw)] = acc4[...]

    mine = full.at[pl.ds(pl.multiple_of(row3, 8), h3), pl.ds(pl.multiple_of(pz * cw, 128), cw)]
    wait_all([send(mine, mine, z_dev(o)) for o in (1, 2, 3)])
    mine = full.at[pl.ds(pl.multiple_of(row3, 8), h3)]
    wait_all([send(mine, mine, x_dev(o)) for o in (1, 2, 3)])
    mine = full.at[pl.ds(pl.multiple_of(row2, 8), h2)]
    wait_all([send(mine, mine, y_dev(o)) for o in (1, 2, 3)])
    mine = full.at[pl.ds(pl.multiple_of(row1, 8), h1)]
    send(mine, mine, core_dev).wait()

    o_ref[...] = full[...]


def allreduce_all(x):
    rows, cols = x.shape
    h1 = rows // 2
    h2 = h1 // 4
    h3 = h2 // 4
    cw = cols // 4
    f32 = jnp.float32
    return pl.pallas_call(
        _allreduce_kernel,
        out_shape=jax.ShapeDtypeStruct((rows, cols), f32),
        in_specs=[pl.BlockSpec(memory_space=pltpu.VMEM)],
        out_specs=pl.BlockSpec(memory_space=pltpu.VMEM),
        scratch_shapes=[
            pltpu.VMEM((h1, cols), f32),
            pltpu.VMEM((h2, cols), f32),
            pltpu.VMEM((h3, cols), f32),
            pltpu.VMEM((h3, cw), f32),
            pltpu.VMEM((h1, cols), f32),
            pltpu.VMEM((3, h2, cols), f32),
            pltpu.VMEM((3, h3, cols), f32),
            pltpu.VMEM((3, h3, cw), f32),
            pltpu.VMEM((rows, cols), f32),
            pltpu.SemaphoreType.DMA((20,)),
            pltpu.SemaphoreType.DMA((20,)),
        ],
        compiler_params=pltpu.CompilerParams(collective_id=0, has_side_effects=True),
    )(x)


def _subspace_kernel(g_ref, b0_ref, o_ref):
    highest = lax.Precision.HIGHEST
    rank = b0_ref.shape[0]
    rows = lax.broadcasted_iota(jnp.int32, (rank, rank), 0)
    cols = lax.broadcasted_iota(jnp.int32, (rank, rank), 1)
    col_idx = lax.broadcasted_iota(jnp.int32, (rank, 1), 0)
    row_idx = lax.broadcasted_iota(jnp.int32, (1, rank), 1)
    eye = jnp.where(rows == cols, 1.0, 0.0).astype(jnp.float32)
    zero = jnp.zeros((rank, rank), jnp.float32)

    def step(j, carry):
        m, e, z = carry
        at_row = rows == j
        row_m = jnp.sum(jnp.where(at_row, m, 0.0), axis=0, keepdims=True)
        col_m = jnp.sum(jnp.where(cols == j, m, 0.0), axis=1, keepdims=True)
        d = jnp.sum(jnp.where(row_idx == j, row_m, 0.0), axis=1, keepdims=True)
        s = lax.rsqrt(d)
        c = jnp.where(col_idx >= j, col_m * s, 0.0)
        r = jnp.where(row_idx >= j, row_m * s, 0.0)
        m = m - c * r
        zr = jnp.sum(jnp.where(at_row, e, 0.0), axis=0, keepdims=True) * s
        e = e - c * zr
        z = jnp.where(at_row, zr, z)
        return m, e, z

    def sweep(_, basis_t):
        block_t = jnp.dot(basis_t, g_ref[...], precision=highest, preferred_element_type=jnp.float32)
        inner = lax.dot_general(block_t, block_t, (((1,), (1,)), ((), ())), precision=highest,
                                preferred_element_type=jnp.float32)
        _, _, l_inv = lax.fori_loop(0, rank, step, (inner, eye, zero))
        return jnp.dot(l_inv, block_t, precision=highest, preferred_element_type=jnp.float32)

    o_ref[...] = lax.fori_loop(0, ITERS, sweep, b0_ref[...])


def subspace_iterate(gram, start_basis):
    basis_t = pl.pallas_call(
        _subspace_kernel,
        out_shape=jax.ShapeDtypeStruct(start_basis.shape[::-1], jnp.float32),
        in_specs=[pl.BlockSpec(memory_space=pltpu.VMEM)] * 2,
        out_specs=pl.BlockSpec(memory_space=pltpu.VMEM),
    )(gram, start_basis.T)
    return basis_t.T


def _gram_kernel(s_ref, o_ref, hi_ref, lo_ref, cross_ref):
    step = pl.program_id(0)
    depth = s_ref.shape[1]
    width = s_ref.shape[2]
    for jj in range(depth):
        x = s_ref[:, jj, :]
        hi = x.astype(jnp.bfloat16)
        lo = (x - hi.astype(jnp.float32)).astype(jnp.bfloat16)
        hi_ref[:, jj * width:(jj + 1) * width] = hi
        lo_ref[:, jj * width:(jj + 1) * width] = lo
    nt = (((1,), (1,)), ((), ()))
    hh = lax.dot_general(hi_ref[...], hi_ref[...], nt, preferred_element_type=jnp.float32)
    hl = lax.dot_general(hi_ref[...], lo_ref[...], nt, preferred_element_type=jnp.float32)

    @pl.when(step == 0)
    def _():
        o_ref[...] = hh
        cross_ref[...] = hl

    @pl.when(step > 0)
    def _():
        o_ref[...] += hh
        cross_ref[...] += hl

    @pl.when(step == pl.num_programs(0) - 1)
    def _():
        o_ref[...] += cross_ref[...] + cross_ref[...].T


def local_gram(slab, depth=8):
    rows, cols, width = slab.shape
    return pl.pallas_call(
        _gram_kernel,
        out_shape=jax.ShapeDtypeStruct((rows, rows), jnp.float32),
        grid=(cols // depth,),
        in_specs=[pl.BlockSpec((rows, depth, width), lambda g: (0, g, 0))],
        out_specs=pl.BlockSpec((rows, rows), lambda g: (0, 0)),
        scratch_shapes=[
            pltpu.VMEM((rows, depth * width), jnp.bfloat16),
            pltpu.VMEM((rows, depth * width), jnp.bfloat16),
            pltpu.VMEM((rows, rows), jnp.float32),
        ],
        compiler_params=pltpu.CompilerParams(vmem_limit_bytes=48 * 1024 * 1024),
    )(slab)


def shards(tensor_slab, start_basis):
    highest = lax.Precision.HIGHEST
    high = lax.Precision.HIGH
    basis = start_basis
    gram_full = allreduce_all(local_gram(tensor_slab))
    basis = subspace_iterate(gram_full, start_basis)
    proj = jnp.einsum("ir,ijl->rjl", basis, tensor_slab, precision=high, preferred_element_type=jnp.float32)
    proj = lax.all_to_all(proj, "wide", split_axis=0, concat_axis=1, tiled=True)
    core_unfold = jnp.transpose(proj, (2, 0, 1))
    return (basis, core_unfold)


def solution(mesh):
    placed = (P(None, "wide", "narrow"), P())
    return jax.shard_map(
        shards,
        mesh=mesh,
        in_specs=placed,
        out_specs=(P(), P("narrow", "wide", None)),
        check_vma=False,
    )
```

```python
import functools

import jax
import jax.numpy as jnp
from jax import lax
from jax.experimental import pallas as pl
from jax.experimental.pallas import tpu as pltpu
from jax.sharding import PartitionSpec as P

I1 = 512
ITERS = 8
MESH = pl.DeviceIdType.MESH


def orthonormal(block, inner):
    lower_factor = jnp.linalg.cholesky(inner)
    return jax.scipy.linalg.solve_triangular(lower_factor, block.T, lower=True).T


def _allreduce_kernel(x_ref, o_ref, acc1, acc2, acc3, acc4, r1, r2, r3, r4, full, send_sems, recv_sems):
    w = lax.axis_index("wide")
    n = lax.axis_index("narrow")
    px, pz = w // 4, w % 4
    py, pc = n // 2, n % 2
    rows, cols = x_ref.shape
    h1 = rows // 2
    h2 = h1 // 4
    h3 = h2 // 4
    cw = cols // 4

    core_dev = (w, py * 2 + (1 - pc))

    def y_dev(o):
        return (w, ((py + o) % 4) * 2 + pc)

    def x_dev(o):
        return (((px + o) % 4) * 4 + pz, n)

    def z_dev(o):
        return (px * 4 + (pz + o) % 4, n)

    partners = [core_dev] + [y_dev(o) for o in (1, 2, 3)] + [x_dev(o) for o in (1, 2, 3)] + [z_dev(o) for o in (1, 2, 3)]
    barrier = pltpu.get_barrier_semaphore()
    for dev in partners:
        pl.semaphore_signal(barrier, inc=1, device_id=dev, device_id_type=MESH)
    pl.semaphore_wait(barrier, len(partners))

    slot = [0]

    def send(src, dst, dev):
        k = slot[0]
        slot[0] += 1
        cp = pltpu.make_async_remote_copy(
            src_ref=src, dst_ref=dst, send_sem=send_sems.at[k], recv_sem=recv_sems.at[k],
            device_id=dev, device_id_type=MESH)
        cp.start()
        return cp

    def wait_all(cps):
        for cp in cps:
            cp.wait()

    cp = send(x_ref.at[pl.ds(pl.multiple_of((1 - pc) * h1, 8), h1)], r1, core_dev)
    cp.wait()
    acc1[...] = x_ref[pl.ds(pl.multiple_of(pc * h1, 8), h1), :] + r1[...]

    cps = []
    for o in (1, 2, 3):
        q = (py + o) % 4
        cps.append(send(acc1.at[pl.ds(pl.multiple_of(q * h2, 8), h2)], r2.at[o - 1], y_dev(o)))
    wait_all(cps)
    acc2[...] = acc1[pl.ds(pl.multiple_of(py * h2, 8), h2), :] + r2[0] + r2[1] + r2[2]

    cps = []
    for o in (1, 2, 3):
        q = (px + o) % 4
        cps.append(send(acc2.at[pl.ds(pl.multiple_of(q * h3, 8), h3)], r3.at[o - 1], x_dev(o)))
    wait_all(cps)
    acc3[...] = acc2[pl.ds(pl.multiple_of(px * h3, 8), h3), :] + r3[0] + r3[1] + r3[2]

    cps = []
    for o in (1, 2, 3):
        q = (pz + o) % 4
        cps.append(send(acc3.at[:, pl.ds(pl.multiple_of(q * cw, 128), cw)], r4.at[o - 1], z_dev(o)))
    wait_all(cps)
    acc4[...] = acc3[:, pl.ds(pl.multiple_of(pz * cw, 128), cw)] + r4[0] + r4[1] + r4[2]

    row1 = pc * h1
    row2 = row1 + py * h2
    row3 = row2 + px * h3
    full[pl.ds(pl.multiple_of(row3, 8), h3), pl.ds(pl.multiple_of(pz * cw, 128), cw)] = acc4[...]

    mine = full.at[pl.ds(pl.multiple_of(row3, 8), h3), pl.ds(pl.multiple_of(pz * cw, 128), cw)]
    wait_all([send(mine, mine, z_dev(o)) for o in (1, 2, 3)])
    mine = full.at[pl.ds(pl.multiple_of(row3, 8), h3)]
    wait_all([send(mine, mine, x_dev(o)) for o in (1, 2, 3)])
    mine = full.at[pl.ds(pl.multiple_of(row2, 8), h2)]
    wait_all([send(mine, mine, y_dev(o)) for o in (1, 2, 3)])
    mine = full.at[pl.ds(pl.multiple_of(row1, 8), h1)]
    send(mine, mine, core_dev).wait()

    o_ref[...] = full[...]


def allreduce_all(x):
    rows, cols = x.shape
    h1 = rows // 2
    h2 = h1 // 4
    h3 = h2 // 4
    cw = cols // 4
    f32 = jnp.float32
    return pl.pallas_call(
        _allreduce_kernel,
        out_shape=jax.ShapeDtypeStruct((rows, cols), f32),
        in_specs=[pl.BlockSpec(memory_space=pltpu.VMEM)],
        out_specs=pl.BlockSpec(memory_space=pltpu.VMEM),
        scratch_shapes=[
            pltpu.VMEM((h1, cols), f32),
            pltpu.VMEM((h2, cols), f32),
            pltpu.VMEM((h3, cols), f32),
            pltpu.VMEM((h3, cw), f32),
            pltpu.VMEM((h1, cols), f32),
            pltpu.VMEM((3, h2, cols), f32),
            pltpu.VMEM((3, h3, cols), f32),
            pltpu.VMEM((3, h3, cw), f32),
            pltpu.VMEM((rows, cols), f32),
            pltpu.SemaphoreType.DMA((20,)),
            pltpu.SemaphoreType.DMA((20,)),
        ],
        compiler_params=pltpu.CompilerParams(collective_id=0, has_side_effects=True),
    )(x)


def _subspace_kernel(g_ref, b0_ref, o_ref):
    highest = lax.Precision.HIGHEST
    rank = b0_ref.shape[0]
    rows = lax.broadcasted_iota(jnp.int32, (rank, rank), 0)
    cols = lax.broadcasted_iota(jnp.int32, (rank, rank), 1)
    col_idx = lax.broadcasted_iota(jnp.int32, (rank, 1), 0)
    row_idx = lax.broadcasted_iota(jnp.int32, (1, rank), 1)
    eye = jnp.where(rows == cols, 1.0, 0.0).astype(jnp.float32)
    zero = jnp.zeros((rank, rank), jnp.float32)

    def step(j, carry):
        m, e, z = carry
        at_row = rows == j
        row_m = jnp.sum(jnp.where(at_row, m, 0.0), axis=0, keepdims=True)
        col_m = jnp.sum(jnp.where(cols == j, m, 0.0), axis=1, keepdims=True)
        d = jnp.sum(jnp.where(row_idx == j, row_m, 0.0), axis=1, keepdims=True)
        s = lax.rsqrt(d)
        c = jnp.where(col_idx >= j, col_m * s, 0.0)
        r = jnp.where(row_idx >= j, row_m * s, 0.0)
        m = m - c * r
        zr = jnp.sum(jnp.where(at_row, e, 0.0), axis=0, keepdims=True) * s
        e = e - c * zr
        z = jnp.where(at_row, zr, z)
        return m, e, z

    def sweep(_, basis_t):
        block_t = jnp.dot(basis_t, g_ref[...], precision=highest, preferred_element_type=jnp.float32)
        inner = lax.dot_general(block_t, block_t, (((1,), (1,)), ((), ())), precision=highest,
                                preferred_element_type=jnp.float32)
        _, _, l_inv = lax.fori_loop(0, rank, step, (inner, eye, zero))
        return jnp.dot(l_inv, block_t, precision=highest, preferred_element_type=jnp.float32)

    o_ref[...] = lax.fori_loop(0, ITERS, sweep, b0_ref[...])


def subspace_iterate(gram, start_basis):
    basis_t = pl.pallas_call(
        _subspace_kernel,
        out_shape=jax.ShapeDtypeStruct(start_basis.shape[::-1], jnp.float32),
        in_specs=[pl.BlockSpec(memory_space=pltpu.VMEM)] * 2,
        out_specs=pl.BlockSpec(memory_space=pltpu.VMEM),
    )(gram, start_basis.T)
    return basis_t.T


def _gram_kernel(s_hbm, o_ref, buf, hi_ref, lo_ref, cross_ref, sems):
    _, cols, width = s_hbm.shape
    slots = buf.shape[0]
    depth = hi_ref.shape[1] // width

    def copy(j):
        return pltpu.make_async_copy(s_hbm.at[:, j, :], buf.at[j % slots], sems.at[j % slots])

    for j in range(slots - 1):
        copy(j).start()
    nt = (((1,), (1,)), ((), ()))
    for g in range(cols // depth):
        for jj in range(depth):
            j = g * depth + jj
            if j + slots - 1 < cols:
                copy(j + slots - 1).start()
            copy(j).wait()
            x = buf[j % slots]
            hi = x.astype(jnp.bfloat16)
            lo = (x - hi.astype(jnp.float32)).astype(jnp.bfloat16)
            hi_ref[:, jj * width:(jj + 1) * width] = hi
            lo_ref[:, jj * width:(jj + 1) * width] = lo
        hh = lax.dot_general(hi_ref[...], hi_ref[...], nt, preferred_element_type=jnp.float32)
        hl = lax.dot_general(hi_ref[...], lo_ref[...], nt, preferred_element_type=jnp.float32)
        if g == 0:
            o_ref[...] = hh
            cross_ref[...] = hl
        else:
            o_ref[...] += hh
            cross_ref[...] += hl
    o_ref[...] += cross_ref[...] + cross_ref[...].T


def local_gram(slab, depth=8, slots=8):
    rows, cols, width = slab.shape
    return pl.pallas_call(
        _gram_kernel,
        out_shape=jax.ShapeDtypeStruct((rows, rows), jnp.float32),
        in_specs=[pl.BlockSpec(memory_space=pl.ANY)],
        out_specs=pl.BlockSpec(memory_space=pltpu.VMEM),
        scratch_shapes=[
            pltpu.VMEM((slots, rows, width), jnp.float32),
            pltpu.VMEM((rows, depth * width), jnp.bfloat16),
            pltpu.VMEM((rows, depth * width), jnp.bfloat16),
            pltpu.VMEM((rows, rows), jnp.float32),
            pltpu.SemaphoreType.DMA((slots,)),
        ],
        compiler_params=pltpu.CompilerParams(vmem_limit_bytes=48 * 1024 * 1024),
    )(slab)

def shards(tensor_slab, start_basis):
    highest = lax.Precision.HIGHEST
    high = lax.Precision.HIGH
    basis = start_basis
    gram_full = allreduce_all(local_gram(tensor_slab))
    basis = subspace_iterate(gram_full, start_basis)
    proj = jnp.einsum("ir,ijl->rjl", basis, tensor_slab, precision=high, preferred_element_type=jnp.float32)
    proj = lax.all_to_all(proj, "wide", split_axis=0, concat_axis=1, tiled=True)
    core_unfold = jnp.transpose(proj, (2, 0, 1))
    return (basis, core_unfold)


def solution(mesh):
    placed = (P(None, "wide", "narrow"), P())
    return jax.shard_map(
        shards,
        mesh=mesh,
        in_specs=placed,
        out_specs=(P(), P("narrow", "wide", None)),
        check_vma=False,
    )
```

```python
import functools

import jax
import jax.numpy as jnp
from jax import lax
from jax.experimental import pallas as pl
from jax.experimental.pallas import tpu as pltpu
from jax.sharding import PartitionSpec as P

I1 = 512
ITERS = 8
MESH = pl.DeviceIdType.MESH


def orthonormal(block, inner):
    lower_factor = jnp.linalg.cholesky(inner)
    return jax.scipy.linalg.solve_triangular(lower_factor, block.T, lower=True).T


def _allreduce_kernel(x_ref, o_ref, acc1, acc2, acc3, acc4, r1, r2, r3, r4, full, send_sems, recv_sems):
    w = lax.axis_index("wide")
    n = lax.axis_index("narrow")
    px, pz = w // 4, w % 4
    py, pc = n // 2, n % 2
    rows, cols = x_ref.shape
    h1 = rows // 2
    h2 = h1 // 4
    h3 = h2 // 4
    cw = cols // 4

    core_dev = (w, py * 2 + (1 - pc))

    def y_dev(o):
        return (w, ((py + o) % 4) * 2 + pc)

    def x_dev(o):
        return (((px + o) % 4) * 4 + pz, n)

    def z_dev(o):
        return (px * 4 + (pz + o) % 4, n)

    partners = [core_dev] + [y_dev(o) for o in (1, 2, 3)] + [x_dev(o) for o in (1, 2, 3)] + [z_dev(o) for o in (1, 2, 3)]
    barrier = pltpu.get_barrier_semaphore()
    for dev in partners:
        pl.semaphore_signal(barrier, inc=1, device_id=dev, device_id_type=MESH)
    pl.semaphore_wait(barrier, len(partners))

    slot = [0]

    def send(src, dst, dev):
        k = slot[0]
        slot[0] += 1
        cp = pltpu.make_async_remote_copy(
            src_ref=src, dst_ref=dst, send_sem=send_sems.at[k], recv_sem=recv_sems.at[k],
            device_id=dev, device_id_type=MESH)
        cp.start()
        return cp

    def wait_all(cps):
        for cp in cps:
            cp.wait()

    cp = send(x_ref.at[pl.ds(pl.multiple_of((1 - pc) * h1, 8), h1)], r1, core_dev)
    cp.wait()
    acc1[...] = x_ref[pl.ds(pl.multiple_of(pc * h1, 8), h1), :] + r1[...]

    cps = []
    for o in (1, 2, 3):
        q = (py + o) % 4
        cps.append(send(acc1.at[pl.ds(pl.multiple_of(q * h2, 8), h2)], r2.at[o - 1], y_dev(o)))
    wait_all(cps)
    acc2[...] = acc1[pl.ds(pl.multiple_of(py * h2, 8), h2), :] + r2[0] + r2[1] + r2[2]

    cps = []
    for o in (1, 2, 3):
        q = (px + o) % 4
        cps.append(send(acc2.at[pl.ds(pl.multiple_of(q * h3, 8), h3)], r3.at[o - 1], x_dev(o)))
    wait_all(cps)
    acc3[...] = acc2[pl.ds(pl.multiple_of(px * h3, 8), h3), :] + r3[0] + r3[1] + r3[2]

    cps = []
    for o in (1, 2, 3):
        q = (pz + o) % 4
        cps.append(send(acc3.at[:, pl.ds(pl.multiple_of(q * cw, 128), cw)], r4.at[o - 1], z_dev(o)))
    wait_all(cps)
    acc4[...] = acc3[:, pl.ds(pl.multiple_of(pz * cw, 128), cw)] + r4[0] + r4[1] + r4[2]

    row1 = pc * h1
    row2 = row1 + py * h2
    row3 = row2 + px * h3
    full[pl.ds(pl.multiple_of(row3, 8), h3), pl.ds(pl.multiple_of(pz * cw, 128), cw)] = acc4[...]

    mine = full.at[pl.ds(pl.multiple_of(row3, 8), h3), pl.ds(pl.multiple_of(pz * cw, 128), cw)]
    wait_all([send(mine, mine, z_dev(o)) for o in (1, 2, 3)])
    mine = full.at[pl.ds(pl.multiple_of(row3, 8), h3)]
    wait_all([send(mine, mine, x_dev(o)) for o in (1, 2, 3)])
    mine = full.at[pl.ds(pl.multiple_of(row2, 8), h2)]
    wait_all([send(mine, mine, y_dev(o)) for o in (1, 2, 3)])
    mine = full.at[pl.ds(pl.multiple_of(row1, 8), h1)]
    send(mine, mine, core_dev).wait()

    o_ref[...] = full[...]


def allreduce_all(x):
    rows, cols = x.shape
    h1 = rows // 2
    h2 = h1 // 4
    h3 = h2 // 4
    cw = cols // 4
    f32 = jnp.float32
    return pl.pallas_call(
        _allreduce_kernel,
        out_shape=jax.ShapeDtypeStruct((rows, cols), f32),
        in_specs=[pl.BlockSpec(memory_space=pltpu.VMEM)],
        out_specs=pl.BlockSpec(memory_space=pltpu.VMEM),
        scratch_shapes=[
            pltpu.VMEM((h1, cols), f32),
            pltpu.VMEM((h2, cols), f32),
            pltpu.VMEM((h3, cols), f32),
            pltpu.VMEM((h3, cw), f32),
            pltpu.VMEM((h1, cols), f32),
            pltpu.VMEM((3, h2, cols), f32),
            pltpu.VMEM((3, h3, cols), f32),
            pltpu.VMEM((3, h3, cw), f32),
            pltpu.VMEM((rows, cols), f32),
            pltpu.SemaphoreType.DMA((20,)),
            pltpu.SemaphoreType.DMA((20,)),
        ],
        compiler_params=pltpu.CompilerParams(collective_id=0, has_side_effects=True),
    )(x)


def _subspace_kernel(g_ref, b0_ref, o_ref):
    highest = lax.Precision.HIGHEST
    rank = b0_ref.shape[0]
    rows = lax.broadcasted_iota(jnp.int32, (rank, rank), 0)
    cols = lax.broadcasted_iota(jnp.int32, (rank, rank), 1)
    col_idx = lax.broadcasted_iota(jnp.int32, (rank, 1), 0)
    row_idx = lax.broadcasted_iota(jnp.int32, (1, rank), 1)
    eye = jnp.where(rows == cols, 1.0, 0.0).astype(jnp.float32)
    zero = jnp.zeros((rank, rank), jnp.float32)

    def step(j, carry):
        m, e, z = carry
        at_row = rows == j
        row_m = jnp.sum(jnp.where(at_row, m, 0.0), axis=0, keepdims=True)
        col_m = jnp.sum(jnp.where(cols == j, m, 0.0), axis=1, keepdims=True)
        d = jnp.sum(jnp.where(row_idx == j, row_m, 0.0), axis=1, keepdims=True)
        s = lax.rsqrt(d)
        c = jnp.where(col_idx >= j, col_m * s, 0.0)
        r = jnp.where(row_idx >= j, row_m * s, 0.0)
        m = m - c * r
        zr = jnp.sum(jnp.where(at_row, e, 0.0), axis=0, keepdims=True) * s
        e = e - c * zr
        z = jnp.where(at_row, zr, z)
        return m, e, z

    def sweep(_, basis_t):
        block_t = jnp.dot(basis_t, g_ref[...], precision=highest, preferred_element_type=jnp.float32)
        inner = lax.dot_general(block_t, block_t, (((1,), (1,)), ((), ())), precision=highest,
                                preferred_element_type=jnp.float32)
        _, _, l_inv = lax.fori_loop(0, rank, step, (inner, eye, zero))
        return jnp.dot(l_inv, block_t, precision=highest, preferred_element_type=jnp.float32)

    o_ref[...] = lax.fori_loop(0, ITERS, sweep, b0_ref[...])


def subspace_iterate(gram, start_basis):
    basis_t = pl.pallas_call(
        _subspace_kernel,
        out_shape=jax.ShapeDtypeStruct(start_basis.shape[::-1], jnp.float32),
        in_specs=[pl.BlockSpec(memory_space=pltpu.VMEM)] * 2,
        out_specs=pl.BlockSpec(memory_space=pltpu.VMEM),
    )(gram, start_basis.T)
    return basis_t.T


def _gram_kernel(s_hbm, o_ref, hi_hbm, lo_hbm, buf, hi_ref, lo_ref, cross_ref, sems, out_sems):
    _, cols, width = s_hbm.shape
    slots = buf.shape[0]
    groups = out_sems.shape[1]
    span = hi_ref.shape[1] // groups
    depth = span // width

    def copy(j):
        return pltpu.make_async_copy(s_hbm.at[:, j, :], buf.at[j % slots], sems.at[j % slots])

    def write_back(g):
        part = pl.ds(g * span, span)
        return (pltpu.make_async_copy(hi_ref.at[:, part], hi_hbm.at[:, part], out_sems.at[0, g]),
                pltpu.make_async_copy(lo_ref.at[:, part], lo_hbm.at[:, part], out_sems.at[1, g]))

    for j in range(slots - 1):
        copy(j).start()
    nt = (((1,), (1,)), ((), ()))
    for g in range(groups):
        for jj in range(depth):
            j = g * depth + jj
            if j + slots - 1 < cols:
                copy(j + slots - 1).start()
            copy(j).wait()
            x = buf[j % slots]
            hi = x.astype(jnp.bfloat16)
            lo = (x - hi.astype(jnp.float32)).astype(jnp.bfloat16)
            hi_ref[:, j * width:(j + 1) * width] = hi
            lo_ref[:, j * width:(j + 1) * width] = lo
        for cp in write_back(g):
            cp.start()
        part = pl.ds(g * span, span)
        hh = lax.dot_general(hi_ref[:, part], hi_ref[:, part], nt, preferred_element_type=jnp.float32)
        hl = lax.dot_general(hi_ref[:, part], lo_ref[:, part], nt, preferred_element_type=jnp.float32)
        if g == 0:
            o_ref[...] = hh
            cross_ref[...] = hl
        else:
            o_ref[...] += hh
            cross_ref[...] += hl
    o_ref[...] += cross_ref[...] + cross_ref[...].T
    for g in range(groups):
        for cp in write_back(g):
            cp.wait()


def local_gram(slab, depth=8, slots=8):
    rows, cols, width = slab.shape
    groups = cols // depth
    flat = jax.ShapeDtypeStruct((rows, cols * width), jnp.bfloat16)
    return pl.pallas_call(
        _gram_kernel,
        out_shape=(jax.ShapeDtypeStruct((rows, rows), jnp.float32), flat, flat),
        in_specs=[pl.BlockSpec(memory_space=pl.ANY)],
        out_specs=(pl.BlockSpec(memory_space=pltpu.VMEM), pl.BlockSpec(memory_space=pl.ANY),
                   pl.BlockSpec(memory_space=pl.ANY)),
        scratch_shapes=[
            pltpu.VMEM((slots, rows, width), jnp.float32),
            pltpu.VMEM((rows, cols * width), jnp.bfloat16),
            pltpu.VMEM((rows, cols * width), jnp.bfloat16),
            pltpu.VMEM((rows, rows), jnp.float32),
            pltpu.SemaphoreType.DMA((slots,)),
            pltpu.SemaphoreType.DMA((2, groups)),
        ],
        compiler_params=pltpu.CompilerParams(vmem_limit_bytes=56 * 1024 * 1024),
    )(slab)

def _project_kernel(b_ref, xh_ref, xl_ref, o_ref):
    f32 = jnp.float32
    b = b_ref[...]
    bh = b.astype(jnp.bfloat16)
    bl = (b - bh.astype(f32)).astype(jnp.bfloat16)
    xh = xh_ref[...]
    o_ref[...] = (jnp.dot(bh, xh, preferred_element_type=f32) + jnp.dot(bh, xl_ref[...], preferred_element_type=f32)
                  + jnp.dot(bl, xh, preferred_element_type=f32))


def project(basis_t, x_hi, x_lo, tile=1024):
    rank, rows = basis_t.shape
    width = x_hi.shape[1]
    return pl.pallas_call(
        _project_kernel,
        out_shape=jax.ShapeDtypeStruct((rank, width), jnp.float32),
        grid=(width // tile,),
        in_specs=[pl.BlockSpec((rank, rows), lambda g: (0, 0)),
                  pl.BlockSpec((rows, tile), lambda g: (0, g)), pl.BlockSpec((rows, tile), lambda g: (0, g))],
        out_specs=pl.BlockSpec((rank, tile), lambda g: (0, g)),
    )(basis_t, x_hi, x_lo)


def shards(wide, tensor_slab, start_basis):
    highest = lax.Precision.HIGHEST
    high = lax.Precision.HIGH
    _, cols, depth = tensor_slab.shape
    basis = start_basis
    gram_part, slab_hi, slab_lo = local_gram(tensor_slab)
    gram_full = allreduce_all(gram_part)
    basis = subspace_iterate(gram_full, start_basis)
    proj = project(basis.T, slab_hi, slab_lo)
    proj = lax.all_to_all(proj, "wide", split_axis=0, concat_axis=0, tiled=True)
    core_unfold = proj.reshape(wide, -1, cols, depth).transpose(3, 1, 0, 2).reshape(depth, -1, wide * cols)
    return (basis, core_unfold)


def solution(mesh):
    placed = (P(None, "wide", "narrow"), P())
    return jax.shard_map(
        functools.partial(shards, mesh.shape["wide"]),
        mesh=mesh,
        in_specs=placed,
        out_specs=(P(), P("narrow", "wide", None)),
        check_vma=False,
    )
```

```python
import functools

import jax
import jax.numpy as jnp
from jax import lax
from jax.experimental import pallas as pl
from jax.experimental.pallas import tpu as pltpu
from jax.sharding import PartitionSpec as P

I1 = 512
ITERS = 8
MESH = pl.DeviceIdType.MESH


def orthonormal(block, inner):
    lower_factor = jnp.linalg.cholesky(inner)
    return jax.scipy.linalg.solve_triangular(lower_factor, block.T, lower=True).T


def _allreduce_kernel(x_ref, o_ref, acc1, acc2, acc3, acc4, r1, r2, r3, r4, full, send_sems, recv_sems):
    w = lax.axis_index("wide")
    n = lax.axis_index("narrow")
    px, pz = w // 4, w % 4
    py, pc = n // 2, n % 2
    rows, cols = x_ref.shape
    h1 = rows // 2
    h2 = h1 // 4
    h3 = h2 // 4
    cw = cols // 4

    core_dev = (w, py * 2 + (1 - pc))

    def y_dev(o):
        return (w, ((py + o) % 4) * 2 + pc)

    def x_dev(o):
        return (((px + o) % 4) * 4 + pz, n)

    def z_dev(o):
        return (px * 4 + (pz + o) % 4, n)

    partners = [core_dev] + [y_dev(o) for o in (1, 2, 3)] + [x_dev(o) for o in (1, 2, 3)] + [z_dev(o) for o in (1, 2, 3)]
    barrier = pltpu.get_barrier_semaphore()
    for dev in partners:
        pl.semaphore_signal(barrier, inc=1, device_id=dev, device_id_type=MESH)
    pl.semaphore_wait(barrier, len(partners))

    slot = [0]

    def send(src, dst, dev):
        k = slot[0]
        slot[0] += 1
        cp = pltpu.make_async_remote_copy(
            src_ref=src, dst_ref=dst, send_sem=send_sems.at[k], recv_sem=recv_sems.at[k],
            device_id=dev, device_id_type=MESH)
        cp.start()
        return cp

    def wait_all(cps):
        for cp in cps:
            cp.wait()

    cp = send(x_ref.at[pl.ds(pl.multiple_of((1 - pc) * h1, 8), h1)], r1, core_dev)
    cp.wait()
    acc1[...] = x_ref[pl.ds(pl.multiple_of(pc * h1, 8), h1), :] + r1[...]

    cps = []
    for o in (1, 2, 3):
        q = (py + o) % 4
        cps.append(send(acc1.at[pl.ds(pl.multiple_of(q * h2, 8), h2)], r2.at[o - 1], y_dev(o)))
    wait_all(cps)
    acc2[...] = acc1[pl.ds(pl.multiple_of(py * h2, 8), h2), :] + r2[0] + r2[1] + r2[2]

    cps = []
    for o in (1, 2, 3):
        q = (px + o) % 4
        cps.append(send(acc2.at[pl.ds(pl.multiple_of(q * h3, 8), h3)], r3.at[o - 1], x_dev(o)))
    wait_all(cps)
    acc3[...] = acc2[pl.ds(pl.multiple_of(px * h3, 8), h3), :] + r3[0] + r3[1] + r3[2]

    cps = []
    for o in (1, 2, 3):
        q = (pz + o) % 4
        cps.append(send(acc3.at[:, pl.ds(pl.multiple_of(q * cw, 128), cw)], r4.at[o - 1], z_dev(o)))
    wait_all(cps)
    acc4[...] = acc3[:, pl.ds(pl.multiple_of(pz * cw, 128), cw)] + r4[0] + r4[1] + r4[2]

    row1 = pc * h1
    row2 = row1 + py * h2
    row3 = row2 + px * h3
    full[pl.ds(pl.multiple_of(row3, 8), h3), pl.ds(pl.multiple_of(pz * cw, 128), cw)] = acc4[...]

    mine = full.at[pl.ds(pl.multiple_of(row3, 8), h3), pl.ds(pl.multiple_of(pz * cw, 128), cw)]
    wait_all([send(mine, mine, z_dev(o)) for o in (1, 2, 3)])
    mine = full.at[pl.ds(pl.multiple_of(row3, 8), h3)]
    wait_all([send(mine, mine, x_dev(o)) for o in (1, 2, 3)])
    mine = full.at[pl.ds(pl.multiple_of(row2, 8), h2)]
    wait_all([send(mine, mine, y_dev(o)) for o in (1, 2, 3)])
    mine = full.at[pl.ds(pl.multiple_of(row1, 8), h1)]
    send(mine, mine, core_dev).wait()

    o_ref[...] = full[...]


def allreduce_all(x):
    rows, cols = x.shape
    h1 = rows // 2
    h2 = h1 // 4
    h3 = h2 // 4
    cw = cols // 4
    f32 = jnp.float32
    return pl.pallas_call(
        _allreduce_kernel,
        out_shape=jax.ShapeDtypeStruct((rows, cols), f32),
        in_specs=[pl.BlockSpec(memory_space=pltpu.VMEM)],
        out_specs=pl.BlockSpec(memory_space=pltpu.VMEM),
        scratch_shapes=[
            pltpu.VMEM((h1, cols), f32),
            pltpu.VMEM((h2, cols), f32),
            pltpu.VMEM((h3, cols), f32),
            pltpu.VMEM((h3, cw), f32),
            pltpu.VMEM((h1, cols), f32),
            pltpu.VMEM((3, h2, cols), f32),
            pltpu.VMEM((3, h3, cols), f32),
            pltpu.VMEM((3, h3, cw), f32),
            pltpu.VMEM((rows, cols), f32),
            pltpu.SemaphoreType.DMA((20,)),
            pltpu.SemaphoreType.DMA((20,)),
        ],
        compiler_params=pltpu.CompilerParams(collective_id=0, has_side_effects=True),
    )(x)


def _subspace_kernel(g_ref, b0_ref, o_ref):
    highest = lax.Precision.HIGHEST
    rank = b0_ref.shape[0]
    rows = lax.broadcasted_iota(jnp.int32, (rank, rank), 0)
    cols = lax.broadcasted_iota(jnp.int32, (rank, rank), 1)
    col_idx = lax.broadcasted_iota(jnp.int32, (rank, 1), 0)
    row_idx = lax.broadcasted_iota(jnp.int32, (1, rank), 1)
    eye = jnp.where(rows == cols, 1.0, 0.0).astype(jnp.float32)
    zero = jnp.zeros((rank, rank), jnp.float32)

    def cholesky_inverse(m):
        e = eye
        z = zero
        for j in range(rank):
            row_m = m[j:j + 1, :]
            col_m = m[:, j:j + 1]
            s = lax.rsqrt(m[j:j + 1, j:j + 1])
            c = jnp.where(col_idx >= j, col_m * s, 0.0)
            r = jnp.where(row_idx >= j, row_m * s, 0.0)
            m = m - c * r
            zr = e[j:j + 1, :] * s
            e = e - c * zr
            z = jnp.where(rows == j, zr, z)
        return z

    def sweep(_, basis_t):
        block_t = jnp.dot(basis_t, g_ref[...], precision=highest, preferred_element_type=jnp.float32)
        inner = lax.dot_general(block_t, block_t, (((1,), (1,)), ((), ())), precision=highest,
                                preferred_element_type=jnp.float32)
        l_inv = cholesky_inverse(inner)
        return jnp.dot(l_inv, block_t, precision=highest, preferred_element_type=jnp.float32)

    o_ref[...] = lax.fori_loop(0, ITERS, sweep, b0_ref[...])


def subspace_iterate(gram, start_basis):
    basis_t = pl.pallas_call(
        _subspace_kernel,
        out_shape=jax.ShapeDtypeStruct(start_basis.shape[::-1], jnp.float32),
        in_specs=[pl.BlockSpec(memory_space=pltpu.VMEM)] * 2,
        out_specs=pl.BlockSpec(memory_space=pltpu.VMEM),
    )(gram, start_basis.T)
    return basis_t.T


def _gram_kernel(s_hbm, o_ref, hi_hbm, lo_hbm, buf, hi_ref, lo_ref, cross_ref, sems, out_sems):
    _, cols, width = s_hbm.shape
    slots = buf.shape[0]
    groups = out_sems.shape[1]
    span = hi_ref.shape[1] // groups
    depth = span // width

    def copy(j):
        return pltpu.make_async_copy(s_hbm.at[:, j, :], buf.at[j % slots], sems.at[j % slots])

    def write_back(g):
        part = pl.ds(g * span, span)
        return (pltpu.make_async_copy(hi_ref.at[:, part], hi_hbm.at[:, part], out_sems.at[0, g]),
                pltpu.make_async_copy(lo_ref.at[:, part], lo_hbm.at[:, part], out_sems.at[1, g]))

    for j in range(slots - 1):
        copy(j).start()
    nt = (((1,), (1,)), ((), ()))
    for g in range(groups):
        for jj in range(depth):
            j = g * depth + jj
            if j + slots - 1 < cols:
                copy(j + slots - 1).start()
            copy(j).wait()
            x = buf[j % slots]
            hi = x.astype(jnp.bfloat16)
            lo = (x - hi.astype(jnp.float32)).astype(jnp.bfloat16)
            hi_ref[:, j * width:(j + 1) * width] = hi
            lo_ref[:, j * width:(j + 1) * width] = lo
        for cp in write_back(g):
            cp.start()
        part = pl.ds(g * span, span)
        hh = lax.dot_general(hi_ref[:, part], hi_ref[:, part], nt, preferred_element_type=jnp.float32)
        hl = lax.dot_general(hi_ref[:, part], lo_ref[:, part], nt, preferred_element_type=jnp.float32)
        if g == 0:
            o_ref[...] = hh
            cross_ref[...] = hl
        else:
            o_ref[...] += hh
            cross_ref[...] += hl
    o_ref[...] += cross_ref[...] + cross_ref[...].T
    for g in range(groups):
        for cp in write_back(g):
            cp.wait()


def local_gram(slab, depth=8, slots=8):
    rows, cols, width = slab.shape
    groups = cols // depth
    flat = jax.ShapeDtypeStruct((rows, cols * width), jnp.bfloat16)
    return pl.pallas_call(
        _gram_kernel,
        out_shape=(jax.ShapeDtypeStruct((rows, rows), jnp.float32), flat, flat),
        in_specs=[pl.BlockSpec(memory_space=pl.ANY)],
        out_specs=(pl.BlockSpec(memory_space=pltpu.VMEM), pl.BlockSpec(memory_space=pl.ANY),
                   pl.BlockSpec(memory_space=pl.ANY)),
        scratch_shapes=[
            pltpu.VMEM((slots, rows, width), jnp.float32),
            pltpu.VMEM((rows, cols * width), jnp.bfloat16),
            pltpu.VMEM((rows, cols * width), jnp.bfloat16),
            pltpu.VMEM((rows, rows), jnp.float32),
            pltpu.SemaphoreType.DMA((slots,)),
            pltpu.SemaphoreType.DMA((2, groups)),
        ],
        compiler_params=pltpu.CompilerParams(vmem_limit_bytes=56 * 1024 * 1024),
    )(slab)

def _project_kernel(b_ref, xh_ref, xl_ref, o_ref):
    f32 = jnp.float32
    b = b_ref[...]
    bh = b.astype(jnp.bfloat16)
    bl = (b - bh.astype(f32)).astype(jnp.bfloat16)
    xh = xh_ref[...]
    o_ref[...] = (jnp.dot(bh, xh, preferred_element_type=f32) + jnp.dot(bh, xl_ref[...], preferred_element_type=f32)
                  + jnp.dot(bl, xh, preferred_element_type=f32))


def project(basis_t, x_hi, x_lo, tile=1024):
    rank, rows = basis_t.shape
    width = x_hi.shape[1]
    return pl.pallas_call(
        _project_kernel,
        out_shape=jax.ShapeDtypeStruct((rank, width), jnp.float32),
        grid=(width // tile,),
        in_specs=[pl.BlockSpec((rank, rows), lambda g: (0, 0)),
                  pl.BlockSpec((rows, tile), lambda g: (0, g)), pl.BlockSpec((rows, tile), lambda g: (0, g))],
        out_specs=pl.BlockSpec((rank, tile), lambda g: (0, g)),
    )(basis_t, x_hi, x_lo)


def shards(wide, tensor_slab, start_basis):
    highest = lax.Precision.HIGHEST
    high = lax.Precision.HIGH
    _, cols, depth = tensor_slab.shape
    basis = start_basis
    gram_part, slab_hi, slab_lo = local_gram(tensor_slab)
    gram_full = allreduce_all(gram_part)
    basis = subspace_iterate(gram_full, start_basis)
    proj = project(basis.T, slab_hi, slab_lo)
    proj = lax.all_to_all(proj, "wide", split_axis=0, concat_axis=0, tiled=True)
    core_unfold = proj.reshape(wide, -1, cols, depth).transpose(3, 1, 0, 2).reshape(depth, -1, wide * cols)
    return (basis, core_unfold)


def solution(mesh):
    placed = (P(None, "wide", "narrow"), P())
    return jax.shard_map(
        functools.partial(shards, mesh.shape["wide"]),
        mesh=mesh,
        in_specs=placed,
        out_specs=(P(), P("narrow", "wide", None)),
        check_vma=False,
    )
```

```python
import functools

import jax
import jax.numpy as jnp
from jax import lax
from jax.experimental import pallas as pl
from jax.experimental.pallas import tpu as pltpu
from jax.sharding import PartitionSpec as P

I1 = 512
ITERS = 8
MESH = pl.DeviceIdType.MESH


def orthonormal(block, inner):
    lower_factor = jnp.linalg.cholesky(inner)
    return jax.scipy.linalg.solve_triangular(lower_factor, block.T, lower=True).T


def _allreduce_kernel(x_ref, o_ref, acc1, acc2, acc3, acc4, r1, r2, r3, r4, full, send_sems, recv_sems):
    w = lax.axis_index("wide")
    n = lax.axis_index("narrow")
    px, pz = w // 4, w % 4
    py, pc = n // 2, n % 2
    rows, cols = x_ref.shape
    h1 = rows // 2
    h2 = h1 // 4
    h3 = h2 // 4
    cw = cols // 4

    core_dev = (w, py * 2 + (1 - pc))

    def y_dev(o):
        return (w, ((py + o) % 4) * 2 + pc)

    def x_dev(o):
        return (((px + o) % 4) * 4 + pz, n)

    def z_dev(o):
        return (px * 4 + (pz + o) % 4, n)

    partners = [core_dev] + [y_dev(o) for o in (1, 2, 3)] + [x_dev(o) for o in (1, 2, 3)] + [z_dev(o) for o in (1, 2, 3)]
    barrier = pltpu.get_barrier_semaphore()
    for dev in partners:
        pl.semaphore_signal(barrier, inc=1, device_id=dev, device_id_type=MESH)
    pl.semaphore_wait(barrier, len(partners))

    slot = [0]

    def send(src, dst, dev):
        k = slot[0]
        slot[0] += 1
        cp = pltpu.make_async_remote_copy(
            src_ref=src, dst_ref=dst, send_sem=send_sems.at[k], recv_sem=recv_sems.at[k],
            device_id=dev, device_id_type=MESH)
        cp.start()
        return cp

    def wait_all(cps):
        for cp in cps:
            cp.wait()

    cp = send(x_ref.at[pl.ds(pl.multiple_of((1 - pc) * h1, 8), h1)], r1, core_dev)
    cp.wait()
    acc1[...] = x_ref[pl.ds(pl.multiple_of(pc * h1, 8), h1), :] + r1[...]

    cps = []
    for o in (1, 2, 3):
        q = (py + o) % 4
        cps.append(send(acc1.at[pl.ds(pl.multiple_of(q * h2, 8), h2)], r2.at[o - 1], y_dev(o)))
    wait_all(cps)
    acc2[...] = acc1[pl.ds(pl.multiple_of(py * h2, 8), h2), :] + r2[0] + r2[1] + r2[2]

    cps = []
    for o in (1, 2, 3):
        q = (px + o) % 4
        cps.append(send(acc2.at[pl.ds(pl.multiple_of(q * h3, 8), h3)], r3.at[o - 1], x_dev(o)))
    wait_all(cps)
    acc3[...] = acc2[pl.ds(pl.multiple_of(px * h3, 8), h3), :] + r3[0] + r3[1] + r3[2]

    cps = []
    for o in (1, 2, 3):
        q = (pz + o) % 4
        cps.append(send(acc3.at[:, pl.ds(pl.multiple_of(q * cw, 128), cw)], r4.at[o - 1], z_dev(o)))
    wait_all(cps)
    acc4[...] = acc3[:, pl.ds(pl.multiple_of(pz * cw, 128), cw)] + r4[0] + r4[1] + r4[2]

    row1 = pc * h1
    row2 = row1 + py * h2
    row3 = row2 + px * h3
    full[pl.ds(pl.multiple_of(row3, 8), h3), pl.ds(pl.multiple_of(pz * cw, 128), cw)] = acc4[...]

    mine = full.at[pl.ds(pl.multiple_of(row3, 8), h3), pl.ds(pl.multiple_of(pz * cw, 128), cw)]
    wait_all([send(mine, mine, z_dev(o)) for o in (1, 2, 3)])
    mine = full.at[pl.ds(pl.multiple_of(row3, 8), h3)]
    wait_all([send(mine, mine, x_dev(o)) for o in (1, 2, 3)])
    mine = full.at[pl.ds(pl.multiple_of(row2, 8), h2)]
    wait_all([send(mine, mine, y_dev(o)) for o in (1, 2, 3)])
    mine = full.at[pl.ds(pl.multiple_of(row1, 8), h1)]
    send(mine, mine, core_dev).wait()

    o_ref[...] = full[...]


def allreduce_all(x):
    rows, cols = x.shape
    h1 = rows // 2
    h2 = h1 // 4
    h3 = h2 // 4
    cw = cols // 4
    f32 = jnp.float32
    return pl.pallas_call(
        _allreduce_kernel,
        out_shape=jax.ShapeDtypeStruct((rows, cols), f32),
        in_specs=[pl.BlockSpec(memory_space=pltpu.VMEM)],
        out_specs=pl.BlockSpec(memory_space=pltpu.VMEM),
        scratch_shapes=[
            pltpu.VMEM((h1, cols), f32),
            pltpu.VMEM((h2, cols), f32),
            pltpu.VMEM((h3, cols), f32),
            pltpu.VMEM((h3, cw), f32),
            pltpu.VMEM((h1, cols), f32),
            pltpu.VMEM((3, h2, cols), f32),
            pltpu.VMEM((3, h3, cols), f32),
            pltpu.VMEM((3, h3, cw), f32),
            pltpu.VMEM((rows, cols), f32),
            pltpu.SemaphoreType.DMA((20,)),
            pltpu.SemaphoreType.DMA((20,)),
        ],
        compiler_params=pltpu.CompilerParams(collective_id=0, has_side_effects=True),
    )(x)


def _subspace_kernel(g_ref, b0_ref, o_ref):
    highest = lax.Precision.HIGHEST
    rank = b0_ref.shape[0]
    rows = lax.broadcasted_iota(jnp.int32, (rank, rank), 0)
    cols = lax.broadcasted_iota(jnp.int32, (rank, rank), 1)
    col_idx = lax.broadcasted_iota(jnp.int32, (rank, 1), 0)
    row_idx = lax.broadcasted_iota(jnp.int32, (1, rank), 1)
    eye = jnp.where(rows == cols, 1.0, 0.0).astype(jnp.float32)
    zero = jnp.zeros((rank, rank), jnp.float32)

    def cholesky_inverse(m):
        e = eye
        z = zero
        for j in range(rank):
            row_m = m[j:j + 1, :]
            col_m = m[:, j:j + 1]
            s = lax.rsqrt(m[j:j + 1, j:j + 1])
            c = jnp.where(col_idx >= j, col_m * s, 0.0)
            r = jnp.where(row_idx >= j, row_m * s, 0.0)
            m = m - c * r
            zr = e[j:j + 1, :] * s
            e = e - c * zr
            z = jnp.where(rows == j, zr, z)
        return z

    def sweep(_, basis_t):
        block_t = jnp.dot(basis_t, g_ref[...], precision=highest, preferred_element_type=jnp.float32)
        inner = lax.dot_general(block_t, block_t, (((1,), (1,)), ((), ())), precision=highest,
                                preferred_element_type=jnp.float32)
        l_inv = cholesky_inverse(inner)
        return jnp.dot(l_inv, block_t, precision=highest, preferred_element_type=jnp.float32)

    o_ref[...] = lax.fori_loop(0, ITERS, sweep, b0_ref[...])


def subspace_iterate(gram, start_basis):
    basis_t = pl.pallas_call(
        _subspace_kernel,
        out_shape=jax.ShapeDtypeStruct(start_basis.shape[::-1], jnp.float32),
        in_specs=[pl.BlockSpec(memory_space=pltpu.VMEM)] * 2,
        out_specs=pl.BlockSpec(memory_space=pltpu.VMEM),
    )(gram, start_basis.T)
    return basis_t.T


def _gram_kernel(s_hbm, o_ref, hi_hbm, lo_hbm, buf, hi_ref, lo_ref, cross_ref, sems, out_sems):
    _, cols, width = s_hbm.shape
    slots = buf.shape[0]
    groups = out_sems.shape[1]
    span = hi_ref.shape[1] // groups
    depth = span // width

    def copy(j):
        return pltpu.make_async_copy(s_hbm.at[:, j, :], buf.at[j % slots], sems.at[j % slots])

    def write_back(g):
        part = pl.ds(g * span, span)
        return (pltpu.make_async_copy(hi_ref.at[:, part], hi_hbm.at[:, part], out_sems.at[0, g]),
                pltpu.make_async_copy(lo_ref.at[:, part], lo_hbm.at[:, part], out_sems.at[1, g]))

    for j in range(slots - 1):
        copy(j).start()
    nt = (((1,), (1,)), ((), ()))
    for g in range(groups):
        for jj in range(depth):
            j = g * depth + jj
            if j + slots - 1 < cols:
                copy(j + slots - 1).start()
            copy(j).wait()
            x = buf[j % slots]
            hi = x.astype(jnp.bfloat16)
            lo = (x - hi.astype(jnp.float32)).astype(jnp.bfloat16)
            hi_ref[:, j * width:(j + 1) * width] = hi
            lo_ref[:, j * width:(j + 1) * width] = lo
        for cp in write_back(g):
            cp.start()
        part = pl.ds(g * span, span)
        hh = lax.dot_general(hi_ref[:, part], hi_ref[:, part], nt, preferred_element_type=jnp.float32)
        hl = lax.dot_general(hi_ref[:, part], lo_ref[:, part], nt, preferred_element_type=jnp.float32)
        if g == 0:
            o_ref[...] = hh
            cross_ref[...] = hl
        else:
            o_ref[...] += hh
            cross_ref[...] += hl
    o_ref[...] += cross_ref[...] + cross_ref[...].T
    for g in range(groups):
        for cp in write_back(g):
            cp.wait()


def local_gram(slab, depth=8, slots=8):
    rows, cols, width = slab.shape
    groups = cols // depth
    flat = jax.ShapeDtypeStruct((rows, cols * width), jnp.bfloat16)
    return pl.pallas_call(
        _gram_kernel,
        out_shape=(jax.ShapeDtypeStruct((rows, rows), jnp.float32), flat, flat),
        in_specs=[pl.BlockSpec(memory_space=pl.ANY)],
        out_specs=(pl.BlockSpec(memory_space=pltpu.VMEM), pl.BlockSpec(memory_space=pl.ANY),
                   pl.BlockSpec(memory_space=pl.ANY)),
        scratch_shapes=[
            pltpu.VMEM((slots, rows, width), jnp.float32),
            pltpu.VMEM((rows, cols * width), jnp.bfloat16),
            pltpu.VMEM((rows, cols * width), jnp.bfloat16),
            pltpu.VMEM((rows, rows), jnp.float32),
            pltpu.SemaphoreType.DMA((slots,)),
            pltpu.SemaphoreType.DMA((2, groups)),
        ],
        compiler_params=pltpu.CompilerParams(vmem_limit_bytes=56 * 1024 * 1024),
    )(slab)

def _project_kernel(b_ref, xh_ref, xl_ref, o_ref):
    f32 = jnp.float32
    b = b_ref[...]
    bh = b.astype(jnp.bfloat16)
    bl = (b - bh.astype(f32)).astype(jnp.bfloat16)
    xh = xh_ref[...]
    res = (jnp.dot(bh, xh, preferred_element_type=f32) + jnp.dot(bh, xl_ref[...], preferred_element_type=f32)
           + jnp.dot(bl, xh, preferred_element_type=f32))
    width = o_ref.shape[2]
    for jj in range(o_ref.shape[1]):
        o_ref[:, jj, :] = res[:, jj * width:(jj + 1) * width]


def project(basis_t, x_hi, x_lo, cols, depth, tile=2048):
    rank, rows = basis_t.shape
    width = x_hi.shape[1]
    per = tile // depth
    return pl.pallas_call(
        _project_kernel,
        out_shape=jax.ShapeDtypeStruct((rank, cols, depth), jnp.float32),
        grid=(width // tile,),
        in_specs=[pl.BlockSpec((rank, rows), lambda g: (0, 0)),
                  pl.BlockSpec((rows, tile), lambda g: (0, g)), pl.BlockSpec((rows, tile), lambda g: (0, g))],
        out_specs=pl.BlockSpec((rank, per, depth), lambda g: (0, g, 0)),
    )(basis_t, x_hi, x_lo)


def shards(wide, tensor_slab, start_basis):
    highest = lax.Precision.HIGHEST
    high = lax.Precision.HIGH
    _, cols, depth = tensor_slab.shape
    basis = start_basis
    gram_part, slab_hi, slab_lo = local_gram(tensor_slab)
    gram_full = allreduce_all(gram_part)
    basis = subspace_iterate(gram_full, start_basis)
    proj = project(basis.T, slab_hi, slab_lo, cols, depth)
    proj = lax.all_to_all(proj, "wide", split_axis=0, concat_axis=1, tiled=True)
    core_unfold = jnp.transpose(proj, (2, 0, 1))
    return (basis, core_unfold)


def solution(mesh):
    placed = (P(None, "wide", "narrow"), P())
    return jax.shard_map(
        functools.partial(shards, mesh.shape["wide"]),
        mesh=mesh,
        in_specs=placed,
        out_specs=(P(), P("narrow", "wide", None)),
        check_vma=False,
    )
```

```python
import functools

import jax
import jax.numpy as jnp
from jax import lax
from jax.experimental import pallas as pl
from jax.experimental.pallas import tpu as pltpu
from jax.sharding import PartitionSpec as P

I1 = 512
ITERS = 8
MESH = pl.DeviceIdType.MESH


def orthonormal(block, inner):
    lower_factor = jnp.linalg.cholesky(inner)
    return jax.scipy.linalg.solve_triangular(lower_factor, block.T, lower=True).T


def _allreduce_kernel(x_ref, o_ref, acc1, acc2, acc3, acc4, r1, r2, r3, r4, full, send_sems, recv_sems):
    w = lax.axis_index("wide")
    n = lax.axis_index("narrow")
    px, pz = w // 4, w % 4
    py, pc = n // 2, n % 2
    rows, cols = x_ref.shape
    h1 = rows // 2
    h2 = h1 // 4
    h3 = h2 // 4
    cw = cols // 4

    core_dev = (w, py * 2 + (1 - pc))

    def y_dev(o):
        return (w, ((py + o) % 4) * 2 + pc)

    def x_dev(o):
        return (((px + o) % 4) * 4 + pz, n)

    def z_dev(o):
        return (px * 4 + (pz + o) % 4, n)

    partners = [core_dev] + [y_dev(o) for o in (1, 2, 3)] + [x_dev(o) for o in (1, 2, 3)] + [z_dev(o) for o in (1, 2, 3)]
    barrier = pltpu.get_barrier_semaphore()
    for dev in partners:
        pl.semaphore_signal(barrier, inc=1, device_id=dev, device_id_type=MESH)
    pl.semaphore_wait(barrier, len(partners))

    slot = [0]

    def send(src, dst, dev):
        k = slot[0]
        slot[0] += 1
        cp = pltpu.make_async_remote_copy(
            src_ref=src, dst_ref=dst, send_sem=send_sems.at[k], recv_sem=recv_sems.at[k],
            device_id=dev, device_id_type=MESH)
        cp.start()
        return cp

    def wait_all(cps):
        for cp in cps:
            cp.wait()

    cp = send(x_ref.at[pl.ds(pl.multiple_of((1 - pc) * h1, 8), h1)], r1, core_dev)
    cp.wait()
    acc1[...] = x_ref[pl.ds(pl.multiple_of(pc * h1, 8), h1), :] + r1[...]

    cps = []
    for o in (1, 2, 3):
        q = (py + o) % 4
        cps.append(send(acc1.at[pl.ds(pl.multiple_of(q * h2, 8), h2)], r2.at[o - 1], y_dev(o)))
    wait_all(cps)
    acc2[...] = acc1[pl.ds(pl.multiple_of(py * h2, 8), h2), :] + r2[0] + r2[1] + r2[2]

    cps = []
    for o in (1, 2, 3):
        q = (px + o) % 4
        cps.append(send(acc2.at[pl.ds(pl.multiple_of(q * h3, 8), h3)], r3.at[o - 1], x_dev(o)))
    wait_all(cps)
    acc3[...] = acc2[pl.ds(pl.multiple_of(px * h3, 8), h3), :] + r3[0] + r3[1] + r3[2]

    cps = []
    for o in (1, 2, 3):
        q = (pz + o) % 4
        cps.append(send(acc3.at[:, pl.ds(pl.multiple_of(q * cw, 128), cw)], r4.at[o - 1], z_dev(o)))
    wait_all(cps)
    acc4[...] = acc3[:, pl.ds(pl.multiple_of(pz * cw, 128), cw)] + r4[0] + r4[1] + r4[2]

    row1 = pc * h1
    row2 = row1 + py * h2
    row3 = row2 + px * h3
    full[pl.ds(pl.multiple_of(row3, 8), h3), pl.ds(pl.multiple_of(pz * cw, 128), cw)] = acc4[...]

    mine = full.at[pl.ds(pl.multiple_of(row3, 8), h3), pl.ds(pl.multiple_of(pz * cw, 128), cw)]
    wait_all([send(mine, mine, z_dev(o)) for o in (1, 2, 3)])
    mine = full.at[pl.ds(pl.multiple_of(row3, 8), h3)]
    wait_all([send(mine, mine, x_dev(o)) for o in (1, 2, 3)])
    mine = full.at[pl.ds(pl.multiple_of(row2, 8), h2)]
    wait_all([send(mine, mine, y_dev(o)) for o in (1, 2, 3)])
    mine = full.at[pl.ds(pl.multiple_of(row1, 8), h1)]
    send(mine, mine, core_dev).wait()

    o_ref[...] = full[...]


def allreduce_all(x):
    rows, cols = x.shape
    h1 = rows // 2
    h2 = h1 // 4
    h3 = h2 // 4
    cw = cols // 4
    f32 = jnp.float32
    return pl.pallas_call(
        _allreduce_kernel,
        out_shape=jax.ShapeDtypeStruct((rows, cols), f32),
        in_specs=[pl.BlockSpec(memory_space=pltpu.VMEM)],
        out_specs=pl.BlockSpec(memory_space=pltpu.VMEM),
        scratch_shapes=[
            pltpu.VMEM((h1, cols), f32),
            pltpu.VMEM((h2, cols), f32),
            pltpu.VMEM((h3, cols), f32),
            pltpu.VMEM((h3, cw), f32),
            pltpu.VMEM((h1, cols), f32),
            pltpu.VMEM((3, h2, cols), f32),
            pltpu.VMEM((3, h3, cols), f32),
            pltpu.VMEM((3, h3, cw), f32),
            pltpu.VMEM((rows, cols), f32),
            pltpu.SemaphoreType.DMA((20,)),
            pltpu.SemaphoreType.DMA((20,)),
        ],
        compiler_params=pltpu.CompilerParams(collective_id=0, has_side_effects=True),
    )(x)


def _subspace_kernel(g_ref, b0_ref, o_ref):
    highest = lax.Precision.HIGHEST
    rank = b0_ref.shape[0]
    rows = lax.broadcasted_iota(jnp.int32, (rank, rank), 0)
    cols = lax.broadcasted_iota(jnp.int32, (rank, rank), 1)
    col_idx = lax.broadcasted_iota(jnp.int32, (rank, 1), 0)
    row_idx = lax.broadcasted_iota(jnp.int32, (1, rank), 1)
    eye = jnp.where(rows == cols, 1.0, 0.0).astype(jnp.float32)
    zero = jnp.zeros((rank, rank), jnp.float32)

    def cholesky_inverse(m):
        e = eye
        z = zero
        for j in range(rank):
            row_m = m[j:j + 1, :]
            col_m = m[:, j:j + 1]
            s = lax.rsqrt(m[j:j + 1, j:j + 1])
            c = jnp.where(col_idx >= j, col_m * s, 0.0)
            r = jnp.where(row_idx >= j, row_m * s, 0.0)
            m = m - c * r
            zr = e[j:j + 1, :] * s
            e = e - c * zr
            z = jnp.where(rows == j, zr, z)
        return z

    def sweep(_, basis_t):
        block_t = jnp.dot(basis_t, g_ref[...], precision=highest, preferred_element_type=jnp.float32)
        inner = lax.dot_general(block_t, block_t, (((1,), (1,)), ((), ())), precision=highest,
                                preferred_element_type=jnp.float32)
        l_inv = cholesky_inverse(inner)
        return jnp.dot(l_inv, block_t, precision=highest, preferred_element_type=jnp.float32)

    o_ref[...] = lax.fori_loop(0, ITERS, sweep, b0_ref[...])


def subspace_iterate(gram, start_basis):
    basis_t = pl.pallas_call(
        _subspace_kernel,
        out_shape=jax.ShapeDtypeStruct(start_basis.shape[::-1], jnp.float32),
        in_specs=[pl.BlockSpec(memory_space=pltpu.VMEM)] * 2,
        out_specs=pl.BlockSpec(memory_space=pltpu.VMEM),
    )(gram, start_basis.T)
    return basis_t.T


def _gram_kernel(s_hbm, o_ref, hi_hbm, lo_hbm, buf, hi_ref, lo_ref, cross_ref, sems, out_sems):
    _, cols, width = s_hbm.shape
    slots = buf.shape[0]
    groups = out_sems.shape[1]
    span = hi_ref.shape[1] // groups
    depth = span // width

    def copy(j):
        return pltpu.make_async_copy(s_hbm.at[:, j, :], buf.at[j % slots], sems.at[j % slots])

    def write_back(g):
        part = pl.ds(g * span, span)
        return (pltpu.make_async_copy(hi_ref.at[:, part], hi_hbm.at[:, part], out_sems.at[0, g]),
                pltpu.make_async_copy(lo_ref.at[:, part], lo_hbm.at[:, part], out_sems.at[1, g]))

    for j in range(slots - 1):
        copy(j).start()
    nt = (((1,), (1,)), ((), ()))
    for g in range(groups):
        for jj in range(depth):
            j = g * depth + jj
            if j + slots - 1 < cols:
                copy(j + slots - 1).start()
            copy(j).wait()
            x = buf[j % slots]
            hi = x.astype(jnp.bfloat16)
            lo = (x - hi.astype(jnp.float32)).astype(jnp.bfloat16)
            hi_ref[:, j * width:(j + 1) * width] = hi
            lo_ref[:, j * width:(j + 1) * width] = lo
        for cp in write_back(g):
            cp.start()
        part = pl.ds(g * span, span)
        hh = lax.dot_general(hi_ref[:, part], hi_ref[:, part], nt, preferred_element_type=jnp.float32)
        hl = lax.dot_general(hi_ref[:, part], lo_ref[:, part], nt, preferred_element_type=jnp.float32)
        if g == 0:
            o_ref[...] = hh
            cross_ref[...] = hl
        else:
            o_ref[...] += hh
            cross_ref[...] += hl
    o_ref[...] += cross_ref[...] + cross_ref[...].T
    for g in range(groups):
        for cp in write_back(g):
            cp.wait()


def local_gram(slab, depth=8, slots=16):
    rows, cols, width = slab.shape
    groups = cols // depth
    flat = jax.ShapeDtypeStruct((rows, cols * width), jnp.bfloat16)
    return pl.pallas_call(
        _gram_kernel,
        out_shape=(jax.ShapeDtypeStruct((rows, rows), jnp.float32), flat, flat),
        in_specs=[pl.BlockSpec(memory_space=pl.ANY)],
        out_specs=(pl.BlockSpec(memory_space=pltpu.VMEM), pl.BlockSpec(memory_space=pl.ANY),
                   pl.BlockSpec(memory_space=pl.ANY)),
        scratch_shapes=[
            pltpu.VMEM((slots, rows, width), jnp.float32),
            pltpu.VMEM((rows, cols * width), jnp.bfloat16),
            pltpu.VMEM((rows, cols * width), jnp.bfloat16),
            pltpu.VMEM((rows, rows), jnp.float32),
            pltpu.SemaphoreType.DMA((slots,)),
            pltpu.SemaphoreType.DMA((2, groups)),
        ],
        compiler_params=pltpu.CompilerParams(vmem_limit_bytes=56 * 1024 * 1024),
    )(slab)

def _project_kernel(b_ref, xh_ref, xl_ref, o_ref):
    f32 = jnp.float32
    b = b_ref[...]
    bh = b.astype(jnp.bfloat16)
    bl = (b - bh.astype(f32)).astype(jnp.bfloat16)
    xh = xh_ref[...]
    res = (jnp.dot(bh, xh, preferred_element_type=f32) + jnp.dot(bh, xl_ref[...], preferred_element_type=f32)
           + jnp.dot(bl, xh, preferred_element_type=f32))
    width = o_ref.shape[2]
    for jj in range(o_ref.shape[1]):
        o_ref[:, jj, :] = res[:, jj * width:(jj + 1) * width]


def project(basis_t, x_hi, x_lo, cols, depth, tile=2048):
    rank, rows = basis_t.shape
    width = x_hi.shape[1]
    per = tile // depth
    return pl.pallas_call(
        _project_kernel,
        out_shape=jax.ShapeDtypeStruct((rank, cols, depth), jnp.float32),
        grid=(width // tile,),
        in_specs=[pl.BlockSpec((rank, rows), lambda g: (0, 0)),
                  pl.BlockSpec((rows, tile), lambda g: (0, g)), pl.BlockSpec((rows, tile), lambda g: (0, g))],
        out_specs=pl.BlockSpec((rank, per, depth), lambda g: (0, g, 0)),
    )(basis_t, x_hi, x_lo)


def shards(wide, tensor_slab, start_basis):
    highest = lax.Precision.HIGHEST
    high = lax.Precision.HIGH
    _, cols, depth = tensor_slab.shape
    basis = start_basis
    gram_part, slab_hi, slab_lo = local_gram(tensor_slab)
    gram_full = allreduce_all(gram_part)
    basis = subspace_iterate(gram_full, start_basis)
    proj = project(basis.T, slab_hi, slab_lo, cols, depth)
    proj = lax.all_to_all(proj, "wide", split_axis=0, concat_axis=1, tiled=True)
    core_unfold = jnp.transpose(proj, (2, 0, 1))
    return (basis, core_unfold)


def solution(mesh):
    placed = (P(None, "wide", "narrow"), P())
    return jax.shard_map(
        functools.partial(shards, mesh.shape["wide"]),
        mesh=mesh,
        in_specs=placed,
        out_specs=(P(), P("narrow", "wide", None)),
        check_vma=False,
    )
```

```python
import functools

import jax
import jax.numpy as jnp
from jax import lax
from jax.experimental import pallas as pl
from jax.experimental.pallas import tpu as pltpu
from jax.sharding import PartitionSpec as P

I1 = 512
ITERS = 8
MESH = pl.DeviceIdType.MESH


def orthonormal(block, inner):
    lower_factor = jnp.linalg.cholesky(inner)
    return jax.scipy.linalg.solve_triangular(lower_factor, block.T, lower=True).T


def _allreduce_kernel(x_ref, o_ref, acc1, acc2, acc3, acc4, r1, r2, r3, r4, full, send_sems, recv_sems):
    w = lax.axis_index("wide")
    n = lax.axis_index("narrow")
    px, pz = w // 4, w % 4
    py, pc = n // 2, n % 2
    rows, cols = x_ref.shape
    h1 = rows // 2
    h2 = h1 // 4
    h3 = h2 // 4
    cw = cols // 4

    core_dev = (w, py * 2 + (1 - pc))

    def y_dev(o):
        return (w, ((py + o) % 4) * 2 + pc)

    def x_dev(o):
        return (((px + o) % 4) * 4 + pz, n)

    def z_dev(o):
        return (px * 4 + (pz + o) % 4, n)

    partners = [core_dev] + [y_dev(o) for o in (1, 2, 3)] + [x_dev(o) for o in (1, 2, 3)] + [z_dev(o) for o in (1, 2, 3)]
    barrier = pltpu.get_barrier_semaphore()
    for dev in partners:
        pl.semaphore_signal(barrier, inc=1, device_id=dev, device_id_type=MESH)
    pl.semaphore_wait(barrier, len(partners))

    slot = [0]

    def send(src, dst, dev):
        k = slot[0]
        slot[0] += 1
        cp = pltpu.make_async_remote_copy(
            src_ref=src, dst_ref=dst, send_sem=send_sems.at[k], recv_sem=recv_sems.at[k],
            device_id=dev, device_id_type=MESH)
        cp.start()
        return cp

    def wait_all(cps):
        for cp in cps:
            cp.wait()

    cp = send(x_ref.at[pl.ds(pl.multiple_of((1 - pc) * h1, 8), h1)], r1, core_dev)
    cp.wait()
    acc1[...] = x_ref[pl.ds(pl.multiple_of(pc * h1, 8), h1), :] + r1[...]

    cps = []
    for o in (1, 2, 3):
        q = (py + o) % 4
        cps.append(send(acc1.at[pl.ds(pl.multiple_of(q * h2, 8), h2)], r2.at[o - 1], y_dev(o)))
    wait_all(cps)
    acc2[...] = acc1[pl.ds(pl.multiple_of(py * h2, 8), h2), :] + r2[0] + r2[1] + r2[2]

    cps = []
    for o in (1, 2, 3):
        q = (px + o) % 4
        cps.append(send(acc2.at[pl.ds(pl.multiple_of(q * h3, 8), h3)], r3.at[o - 1], x_dev(o)))
    wait_all(cps)
    acc3[...] = acc2[pl.ds(pl.multiple_of(px * h3, 8), h3), :] + r3[0] + r3[1] + r3[2]

    cps = []
    for o in (1, 2, 3):
        q = (pz + o) % 4
        cps.append(send(acc3.at[:, pl.ds(pl.multiple_of(q * cw, 128), cw)], r4.at[o - 1], z_dev(o)))
    wait_all(cps)
    acc4[...] = acc3[:, pl.ds(pl.multiple_of(pz * cw, 128), cw)] + r4[0] + r4[1] + r4[2]

    row1 = pc * h1
    row2 = row1 + py * h2
    row3 = row2 + px * h3
    full[pl.ds(pl.multiple_of(row3, 8), h3), pl.ds(pl.multiple_of(pz * cw, 128), cw)] = acc4[...]

    mine = full.at[pl.ds(pl.multiple_of(row3, 8), h3), pl.ds(pl.multiple_of(pz * cw, 128), cw)]
    wait_all([send(mine, mine, z_dev(o)) for o in (1, 2, 3)])
    mine = full.at[pl.ds(pl.multiple_of(row3, 8), h3)]
    wait_all([send(mine, mine, x_dev(o)) for o in (1, 2, 3)])
    mine = full.at[pl.ds(pl.multiple_of(row2, 8), h2)]
    wait_all([send(mine, mine, y_dev(o)) for o in (1, 2, 3)])
    mine = full.at[pl.ds(pl.multiple_of(row1, 8), h1)]
    send(mine, mine, core_dev).wait()

    o_ref[...] = full[...]


def allreduce_all(x):
    rows, cols = x.shape
    h1 = rows // 2
    h2 = h1 // 4
    h3 = h2 // 4
    cw = cols // 4
    f32 = jnp.float32
    return pl.pallas_call(
        _allreduce_kernel,
        out_shape=jax.ShapeDtypeStruct((rows, cols), f32),
        in_specs=[pl.BlockSpec(memory_space=pltpu.VMEM)],
        out_specs=pl.BlockSpec(memory_space=pltpu.VMEM),
        scratch_shapes=[
            pltpu.VMEM((h1, cols), f32),
            pltpu.VMEM((h2, cols), f32),
            pltpu.VMEM((h3, cols), f32),
            pltpu.VMEM((h3, cw), f32),
            pltpu.VMEM((h1, cols), f32),
            pltpu.VMEM((3, h2, cols), f32),
            pltpu.VMEM((3, h3, cols), f32),
            pltpu.VMEM((3, h3, cw), f32),
            pltpu.VMEM((rows, cols), f32),
            pltpu.SemaphoreType.DMA((20,)),
            pltpu.SemaphoreType.DMA((20,)),
        ],
        compiler_params=pltpu.CompilerParams(collective_id=0, has_side_effects=True),
    )(x)


def _subspace_kernel(g_ref, b0_ref, o_ref):
    highest = lax.Precision.HIGHEST
    rank = b0_ref.shape[0]
    rows = lax.broadcasted_iota(jnp.int32, (rank, rank), 0)
    cols = lax.broadcasted_iota(jnp.int32, (rank, rank), 1)
    col_idx = lax.broadcasted_iota(jnp.int32, (rank, 1), 0)
    row_idx = lax.broadcasted_iota(jnp.int32, (1, rank), 1)
    eye = jnp.where(rows == cols, 1.0, 0.0).astype(jnp.float32)
    zero = jnp.zeros((rank, rank), jnp.float32)

    def cholesky_inverse(m):
        e = eye
        z = zero
        for j in range(0, rank, 2):
            k = j + 1
            s0 = lax.rsqrt(m[j:j + 1, j:j + 1])
            t = m[j:j + 1, k:k + 1] * s0
            c0 = jnp.where(col_idx >= j, m[:, j:j + 1] * s0, 0.0)
            r0 = jnp.where(row_idx >= j, m[j:j + 1, :] * s0, 0.0)
            s1 = lax.rsqrt(m[k:k + 1, k:k + 1] - t * t)
            c1 = jnp.where(col_idx >= k, (m[:, k:k + 1] - c0 * t) * s1, 0.0)
            r1 = jnp.where(row_idx >= k, (m[k:k + 1, :] - t * r0) * s1, 0.0)
            m = m - c0 * r0 - c1 * r1
            zj = e[j:j + 1, :] * s0
            zk = (e[k:k + 1, :] - t * zj) * s1
            e = e - c0 * zj - c1 * zk
            z = jnp.where(rows == j, zj, jnp.where(rows == k, zk, z))
        return z

    def sweep(_, basis_t):
        block_t = jnp.dot(basis_t, g_ref[...], precision=highest, preferred_element_type=jnp.float32)
        inner = lax.dot_general(block_t, block_t, (((1,), (1,)), ((), ())), precision=highest,
                                preferred_element_type=jnp.float32)
        l_inv = cholesky_inverse(inner)
        return jnp.dot(l_inv, block_t, precision=highest, preferred_element_type=jnp.float32)

    o_ref[...] = lax.fori_loop(0, ITERS, sweep, b0_ref[...])


def subspace_iterate(gram, start_basis):
    basis_t = pl.pallas_call(
        _subspace_kernel,
        out_shape=jax.ShapeDtypeStruct(start_basis.shape[::-1], jnp.float32),
        in_specs=[pl.BlockSpec(memory_space=pltpu.VMEM)] * 2,
        out_specs=pl.BlockSpec(memory_space=pltpu.VMEM),
    )(gram, start_basis.T)
    return basis_t.T


def _gram_kernel(s_hbm, o_ref, hi_hbm, lo_hbm, buf, hi_ref, lo_ref, cross_ref, sems, out_sems):
    _, cols, width = s_hbm.shape
    slots = buf.shape[0]
    groups = out_sems.shape[1]
    span = hi_ref.shape[1] // groups
    depth = span // width

    def copy(j):
        return pltpu.make_async_copy(s_hbm.at[:, j, :], buf.at[j % slots], sems.at[j % slots])

    def write_back(g):
        part = pl.ds(g * span, span)
        return (pltpu.make_async_copy(hi_ref.at[:, part], hi_hbm.at[:, part], out_sems.at[0, g]),
                pltpu.make_async_copy(lo_ref.at[:, part], lo_hbm.at[:, part], out_sems.at[1, g]))

    for j in range(slots - 1):
        copy(j).start()
    nt = (((1,), (1,)), ((), ()))
    for g in range(groups):
        for jj in range(depth):
            j = g * depth + jj
            if j + slots - 1 < cols:
                copy(j + slots - 1).start()
            copy(j).wait()
            x = buf[j % slots]
            hi = x.astype(jnp.bfloat16)
            lo = (x - hi.astype(jnp.float32)).astype(jnp.bfloat16)
            hi_ref[:, j * width:(j + 1) * width] = hi
            lo_ref[:, j * width:(j + 1) * width] = lo
        for cp in write_back(g):
            cp.start()
        part = pl.ds(g * span, span)
        hh = lax.dot_general(hi_ref[:, part], hi_ref[:, part], nt, preferred_element_type=jnp.float32)
        hl = lax.dot_general(hi_ref[:, part], lo_ref[:, part], nt, preferred_element_type=jnp.float32)
        if g == 0:
            o_ref[...] = hh
            cross_ref[...] = hl
        else:
            o_ref[...] += hh
            cross_ref[...] += hl
    o_ref[...] += cross_ref[...] + cross_ref[...].T
    for g in range(groups):
        for cp in write_back(g):
            cp.wait()


def local_gram(slab, depth=8, slots=16):
    rows, cols, width = slab.shape
    groups = cols // depth
    flat = jax.ShapeDtypeStruct((rows, cols * width), jnp.bfloat16)
    return pl.pallas_call(
        _gram_kernel,
        out_shape=(jax.ShapeDtypeStruct((rows, rows), jnp.float32), flat, flat),
        in_specs=[pl.BlockSpec(memory_space=pl.ANY)],
        out_specs=(pl.BlockSpec(memory_space=pltpu.VMEM), pl.BlockSpec(memory_space=pl.ANY),
                   pl.BlockSpec(memory_space=pl.ANY)),
        scratch_shapes=[
            pltpu.VMEM((slots, rows, width), jnp.float32),
            pltpu.VMEM((rows, cols * width), jnp.bfloat16),
            pltpu.VMEM((rows, cols * width), jnp.bfloat16),
            pltpu.VMEM((rows, rows), jnp.float32),
            pltpu.SemaphoreType.DMA((slots,)),
            pltpu.SemaphoreType.DMA((2, groups)),
        ],
        compiler_params=pltpu.CompilerParams(vmem_limit_bytes=56 * 1024 * 1024),
    )(slab)

def _project_kernel(b_ref, xh_ref, xl_ref, o_ref):
    f32 = jnp.float32
    b = b_ref[...]
    bh = b.astype(jnp.bfloat16)
    bl = (b - bh.astype(f32)).astype(jnp.bfloat16)
    xh = xh_ref[...]
    res = (jnp.dot(bh, xh, preferred_element_type=f32) + jnp.dot(bh, xl_ref[...], preferred_element_type=f32)
           + jnp.dot(bl, xh, preferred_element_type=f32))
    width = o_ref.shape[2]
    for jj in range(o_ref.shape[1]):
        o_ref[:, jj, :] = res[:, jj * width:(jj + 1) * width]


def project(basis_t, x_hi, x_lo, cols, depth, tile=2048):
    rank, rows = basis_t.shape
    width = x_hi.shape[1]
    per = tile // depth
    return pl.pallas_call(
        _project_kernel,
        out_shape=jax.ShapeDtypeStruct((rank, cols, depth), jnp.float32),
        grid=(width // tile,),
        in_specs=[pl.BlockSpec((rank, rows), lambda g: (0, 0)),
                  pl.BlockSpec((rows, tile), lambda g: (0, g)), pl.BlockSpec((rows, tile), lambda g: (0, g))],
        out_specs=pl.BlockSpec((rank, per, depth), lambda g: (0, g, 0)),
    )(basis_t, x_hi, x_lo)


def shards(wide, tensor_slab, start_basis):
    highest = lax.Precision.HIGHEST
    high = lax.Precision.HIGH
    _, cols, depth = tensor_slab.shape
    basis = start_basis
    gram_part, slab_hi, slab_lo = local_gram(tensor_slab)
    gram_full = allreduce_all(gram_part)
    basis = subspace_iterate(gram_full, start_basis)
    proj = project(basis.T, slab_hi, slab_lo, cols, depth)
    proj = lax.all_to_all(proj, "wide", split_axis=0, concat_axis=1, tiled=True)
    core_unfold = jnp.transpose(proj, (2, 0, 1))
    return (basis, core_unfold)


def solution(mesh):
    placed = (P(None, "wide", "narrow"), P())
    return jax.shard_map(
        functools.partial(shards, mesh.shape["wide"]),
        mesh=mesh,
        in_specs=placed,
        out_specs=(P(), P("narrow", "wide", None)),
        check_vma=False,
    )
```

```python
import functools

import jax
import jax.numpy as jnp
from jax import lax
from jax.experimental import pallas as pl
from jax.experimental.pallas import tpu as pltpu
from jax.sharding import PartitionSpec as P

I1 = 512
ITERS = 8
MESH = pl.DeviceIdType.MESH


def orthonormal(block, inner):
    lower_factor = jnp.linalg.cholesky(inner)
    return jax.scipy.linalg.solve_triangular(lower_factor, block.T, lower=True).T


def _allreduce_kernel(x_ref, o_ref, acc1, acc2, acc3, acc4, r1, r2, r3, r4, full, send_sems, recv_sems):
    w = lax.axis_index("wide")
    n = lax.axis_index("narrow")
    px, pz = w // 4, w % 4
    py, pc = n // 2, n % 2
    rows, cols = x_ref.shape
    h1 = rows // 2
    h2 = h1 // 4
    h3 = h2 // 4
    cw = cols // 4

    core_dev = (w, py * 2 + (1 - pc))

    def y_dev(o):
        return (w, ((py + o) % 4) * 2 + pc)

    def x_dev(o):
        return (((px + o) % 4) * 4 + pz, n)

    def z_dev(o):
        return (px * 4 + (pz + o) % 4, n)

    partners = [core_dev] + [y_dev(o) for o in (1, 2, 3)] + [x_dev(o) for o in (1, 2, 3)] + [z_dev(o) for o in (1, 2, 3)]
    barrier = pltpu.get_barrier_semaphore()
    for dev in partners:
        pl.semaphore_signal(barrier, inc=1, device_id=dev, device_id_type=MESH)
    pl.semaphore_wait(barrier, len(partners))

    slot = [0]

    def send(src, dst, dev):
        k = slot[0]
        slot[0] += 1
        cp = pltpu.make_async_remote_copy(
            src_ref=src, dst_ref=dst, send_sem=send_sems.at[k], recv_sem=recv_sems.at[k],
            device_id=dev, device_id_type=MESH)
        cp.start()
        return cp

    def wait_all(cps):
        for cp in cps:
            cp.wait()

    cp = send(x_ref.at[pl.ds(pl.multiple_of((1 - pc) * h1, 8), h1)], r1, core_dev)
    cp.wait()
    acc1[...] = x_ref[pl.ds(pl.multiple_of(pc * h1, 8), h1), :] + r1[...]

    cps = []
    for o in (1, 2, 3):
        q = (py + o) % 4
        cps.append(send(acc1.at[pl.ds(pl.multiple_of(q * h2, 8), h2)], r2.at[o - 1], y_dev(o)))
    wait_all(cps)
    acc2[...] = acc1[pl.ds(pl.multiple_of(py * h2, 8), h2), :] + r2[0] + r2[1] + r2[2]

    cps = []
    for o in (1, 2, 3):
        q = (px + o) % 4
        cps.append(send(acc2.at[pl.ds(pl.multiple_of(q * h3, 8), h3)], r3.at[o - 1], x_dev(o)))
    wait_all(cps)
    acc3[...] = acc2[pl.ds(pl.multiple_of(px * h3, 8), h3), :] + r3[0] + r3[1] + r3[2]

    cps = []
    for o in (1, 2, 3):
        q = (pz + o) % 4
        cps.append(send(acc3.at[:, pl.ds(pl.multiple_of(q * cw, 128), cw)], r4.at[o - 1], z_dev(o)))
    wait_all(cps)
    acc4[...] = acc3[:, pl.ds(pl.multiple_of(pz * cw, 128), cw)] + r4[0] + r4[1] + r4[2]

    row1 = pc * h1
    row2 = row1 + py * h2
    row3 = row2 + px * h3
    full[pl.ds(pl.multiple_of(row3, 8), h3), pl.ds(pl.multiple_of(pz * cw, 128), cw)] = acc4[...]

    mine = full.at[pl.ds(pl.multiple_of(row3, 8), h3), pl.ds(pl.multiple_of(pz * cw, 128), cw)]
    wait_all([send(mine, mine, z_dev(o)) for o in (1, 2, 3)])
    mine = full.at[pl.ds(pl.multiple_of(row3, 8), h3)]
    wait_all([send(mine, mine, x_dev(o)) for o in (1, 2, 3)])
    mine = full.at[pl.ds(pl.multiple_of(row2, 8), h2)]
    wait_all([send(mine, mine, y_dev(o)) for o in (1, 2, 3)])
    mine = full.at[pl.ds(pl.multiple_of(row1, 8), h1)]
    send(mine, mine, core_dev).wait()

    o_ref[...] = full[...]


def allreduce_all(x):
    rows, cols = x.shape
    h1 = rows // 2
    h2 = h1 // 4
    h3 = h2 // 4
    cw = cols // 4
    f32 = jnp.float32
    return pl.pallas_call(
        _allreduce_kernel,
        out_shape=jax.ShapeDtypeStruct((rows, cols), f32),
        in_specs=[pl.BlockSpec(memory_space=pltpu.VMEM)],
        out_specs=pl.BlockSpec(memory_space=pltpu.VMEM),
        scratch_shapes=[
            pltpu.VMEM((h1, cols), f32),
            pltpu.VMEM((h2, cols), f32),
            pltpu.VMEM((h3, cols), f32),
            pltpu.VMEM((h3, cw), f32),
            pltpu.VMEM((h1, cols), f32),
            pltpu.VMEM((3, h2, cols), f32),
            pltpu.VMEM((3, h3, cols), f32),
            pltpu.VMEM((3, h3, cw), f32),
            pltpu.VMEM((rows, cols), f32),
            pltpu.SemaphoreType.DMA((20,)),
            pltpu.SemaphoreType.DMA((20,)),
        ],
        compiler_params=pltpu.CompilerParams(collective_id=0, has_side_effects=True),
    )(x)


def _subspace_kernel(g_ref, b0_ref, o_ref):
    highest = lax.Precision.HIGH
    rank = b0_ref.shape[0]
    rows = lax.broadcasted_iota(jnp.int32, (rank, rank), 0)
    cols = lax.broadcasted_iota(jnp.int32, (rank, rank), 1)
    col_idx = lax.broadcasted_iota(jnp.int32, (rank, 1), 0)
    row_idx = lax.broadcasted_iota(jnp.int32, (1, rank), 1)
    eye = jnp.where(rows == cols, 1.0, 0.0).astype(jnp.float32)
    zero = jnp.zeros((rank, rank), jnp.float32)

    def cholesky_inverse(m):
        e = eye
        z = zero
        for j in range(rank):
            row_m = m[j:j + 1, :]
            col_m = m[:, j:j + 1]
            s = lax.rsqrt(m[j:j + 1, j:j + 1])
            c = jnp.where(col_idx >= j, col_m * s, 0.0)
            r = jnp.where(row_idx >= j, row_m * s, 0.0)
            m = m - c * r
            zr = e[j:j + 1, :] * s
            e = e - c * zr
            z = jnp.where(rows == j, zr, z)
        return z

    def sweep(_, basis_t):
        block_t = jnp.dot(basis_t, g_ref[...], precision=highest, preferred_element_type=jnp.float32)
        inner = lax.dot_general(block_t, block_t, (((1,), (1,)), ((), ())), precision=highest,
                                preferred_element_type=jnp.float32)
        l_inv = cholesky_inverse(inner)
        return jnp.dot(l_inv, block_t, precision=highest, preferred_element_type=jnp.float32)

    o_ref[...] = lax.fori_loop(0, ITERS, sweep, b0_ref[...])


def subspace_iterate(gram, start_basis):
    basis_t = pl.pallas_call(
        _subspace_kernel,
        out_shape=jax.ShapeDtypeStruct(start_basis.shape[::-1], jnp.float32),
        in_specs=[pl.BlockSpec(memory_space=pltpu.VMEM)] * 2,
        out_specs=pl.BlockSpec(memory_space=pltpu.VMEM),
    )(gram, start_basis.T)
    return basis_t.T


def _gram_kernel(s_hbm, o_ref, hi_hbm, lo_hbm, buf, hi_ref, lo_ref, cross_ref, sems, out_sems):
    _, cols, width = s_hbm.shape
    slots = buf.shape[0]
    groups = out_sems.shape[1]
    span = hi_ref.shape[1] // groups
    depth = span // width

    def copy(j):
        return pltpu.make_async_copy(s_hbm.at[:, j, :], buf.at[j % slots], sems.at[j % slots])

    def write_back(g):
        part = pl.ds(g * span, span)
        return (pltpu.make_async_copy(hi_ref.at[:, part], hi_hbm.at[:, part], out_sems.at[0, g]),
                pltpu.make_async_copy(lo_ref.at[:, part], lo_hbm.at[:, part], out_sems.at[1, g]))

    for j in range(slots - 1):
        copy(j).start()
    nt = (((1,), (1,)), ((), ()))
    for g in range(groups):
        for jj in range(depth):
            j = g * depth + jj
            if j + slots - 1 < cols:
                copy(j + slots - 1).start()
            copy(j).wait()
            x = buf[j % slots]
            hi = x.astype(jnp.bfloat16)
            lo = (x - hi.astype(jnp.float32)).astype(jnp.bfloat16)
            hi_ref[:, j * width:(j + 1) * width] = hi
            lo_ref[:, j * width:(j + 1) * width] = lo
        for cp in write_back(g):
            cp.start()
        part = pl.ds(g * span, span)
        hh = lax.dot_general(hi_ref[:, part], hi_ref[:, part], nt, preferred_element_type=jnp.float32)
        hl = lax.dot_general(hi_ref[:, part], lo_ref[:, part], nt, preferred_element_type=jnp.float32)
        if g == 0:
            o_ref[...] = hh
            cross_ref[...] = hl
        else:
            o_ref[...] += hh
            cross_ref[...] += hl
    o_ref[...] += cross_ref[...] + cross_ref[...].T
    for g in range(groups):
        for cp in write_back(g):
            cp.wait()


def local_gram(slab, depth=8, slots=16):
    rows, cols, width = slab.shape
    groups = cols // depth
    flat = jax.ShapeDtypeStruct((rows, cols * width), jnp.bfloat16)
    return pl.pallas_call(
        _gram_kernel,
        out_shape=(jax.ShapeDtypeStruct((rows, rows), jnp.float32), flat, flat),
        in_specs=[pl.BlockSpec(memory_space=pl.ANY)],
        out_specs=(pl.BlockSpec(memory_space=pltpu.VMEM), pl.BlockSpec(memory_space=pl.ANY),
                   pl.BlockSpec(memory_space=pl.ANY)),
        scratch_shapes=[
            pltpu.VMEM((slots, rows, width), jnp.float32),
            pltpu.VMEM((rows, cols * width), jnp.bfloat16),
            pltpu.VMEM((rows, cols * width), jnp.bfloat16),
            pltpu.VMEM((rows, rows), jnp.float32),
            pltpu.SemaphoreType.DMA((slots,)),
            pltpu.SemaphoreType.DMA((2, groups)),
        ],
        compiler_params=pltpu.CompilerParams(vmem_limit_bytes=56 * 1024 * 1024),
    )(slab)

def _project_kernel(b_ref, xh_ref, xl_ref, o_ref):
    f32 = jnp.float32
    b = b_ref[...]
    bh = b.astype(jnp.bfloat16)
    bl = (b - bh.astype(f32)).astype(jnp.bfloat16)
    xh = xh_ref[...]
    res = (jnp.dot(bh, xh, preferred_element_type=f32) + jnp.dot(bh, xl_ref[...], preferred_element_type=f32)
           + jnp.dot(bl, xh, preferred_element_type=f32))
    width = o_ref.shape[2]
    for jj in range(o_ref.shape[1]):
        o_ref[:, jj, :] = res[:, jj * width:(jj + 1) * width]


def project(basis_t, x_hi, x_lo, cols, depth, tile=2048):
    rank, rows = basis_t.shape
    width = x_hi.shape[1]
    per = tile // depth
    return pl.pallas_call(
        _project_kernel,
        out_shape=jax.ShapeDtypeStruct((rank, cols, depth), jnp.float32),
        grid=(width // tile,),
        in_specs=[pl.BlockSpec((rank, rows), lambda g: (0, 0)),
                  pl.BlockSpec((rows, tile), lambda g: (0, g)), pl.BlockSpec((rows, tile), lambda g: (0, g))],
        out_specs=pl.BlockSpec((rank, per, depth), lambda g: (0, g, 0)),
    )(basis_t, x_hi, x_lo)


def shards(wide, tensor_slab, start_basis):
    highest = lax.Precision.HIGHEST
    high = lax.Precision.HIGH
    _, cols, depth = tensor_slab.shape
    basis = start_basis
    gram_part, slab_hi, slab_lo = local_gram(tensor_slab)
    gram_full = allreduce_all(gram_part)
    basis = subspace_iterate(gram_full, start_basis)
    proj = project(basis.T, slab_hi, slab_lo, cols, depth)
    proj = lax.all_to_all(proj, "wide", split_axis=0, concat_axis=1, tiled=True)
    core_unfold = jnp.transpose(proj, (2, 0, 1))
    return (basis, core_unfold)


def solution(mesh):
    placed = (P(None, "wide", "narrow"), P())
    return jax.shard_map(
        functools.partial(shards, mesh.shape["wide"]),
        mesh=mesh,
        in_specs=placed,
        out_specs=(P(), P("narrow", "wide", None)),
        check_vma=False,
    )
```

```python
import functools

import jax
import jax.numpy as jnp
from jax import lax
from jax.experimental import pallas as pl
from jax.experimental.pallas import tpu as pltpu
from jax.sharding import PartitionSpec as P

I1 = 512
ITERS = 8
MESH = pl.DeviceIdType.MESH


def orthonormal(block, inner):
    lower_factor = jnp.linalg.cholesky(inner)
    return jax.scipy.linalg.solve_triangular(lower_factor, block.T, lower=True).T


def _allreduce_kernel(x_ref, o_ref, acc1, acc2, acc3, acc4, r1, r2, r3, r4, full, send_sems, recv_sems):
    w = lax.axis_index("wide")
    n = lax.axis_index("narrow")
    px, pz = w // 4, w % 4
    py, pc = n // 2, n % 2
    rows, cols = x_ref.shape
    h1 = rows // 2
    h2 = h1 // 4
    h3 = h2 // 4
    cw = cols // 4

    core_dev = (w, py * 2 + (1 - pc))

    def y_dev(o):
        return (w, ((py + o) % 4) * 2 + pc)

    def x_dev(o):
        return (((px + o) % 4) * 4 + pz, n)

    def z_dev(o):
        return (px * 4 + (pz + o) % 4, n)

    partners = [core_dev] + [y_dev(o) for o in (1, 2, 3)] + [x_dev(o) for o in (1, 2, 3)] + [z_dev(o) for o in (1, 2, 3)]
    barrier = pltpu.get_barrier_semaphore()
    for dev in partners:
        pl.semaphore_signal(barrier, inc=1, device_id=dev, device_id_type=MESH)
    pl.semaphore_wait(barrier, len(partners))

    slot = [0]

    def send(src, dst, dev):
        k = slot[0]
        slot[0] += 1
        cp = pltpu.make_async_remote_copy(
            src_ref=src, dst_ref=dst, send_sem=send_sems.at[k], recv_sem=recv_sems.at[k],
            device_id=dev, device_id_type=MESH)
        cp.start()
        return cp

    def wait_all(cps):
        for cp in cps:
            cp.wait()

    cp = send(x_ref.at[pl.ds(pl.multiple_of((1 - pc) * h1, 8), h1)], r1, core_dev)
    cp.wait()
    acc1[...] = x_ref[pl.ds(pl.multiple_of(pc * h1, 8), h1), :] + r1[...]

    cps = []
    for o in (1, 2, 3):
        q = (py + o) % 4
        cps.append(send(acc1.at[pl.ds(pl.multiple_of(q * h2, 8), h2)], r2.at[o - 1], y_dev(o)))
    wait_all(cps)
    acc2[...] = acc1[pl.ds(pl.multiple_of(py * h2, 8), h2), :] + r2[0] + r2[1] + r2[2]

    cps = []
    for o in (1, 2, 3):
        q = (px + o) % 4
        cps.append(send(acc2.at[pl.ds(pl.multiple_of(q * h3, 8), h3)], r3.at[o - 1], x_dev(o)))
    wait_all(cps)
    acc3[...] = acc2[pl.ds(pl.multiple_of(px * h3, 8), h3), :] + r3[0] + r3[1] + r3[2]

    cps = []
    for o in (1, 2, 3):
        q = (pz + o) % 4
        cps.append(send(acc3.at[:, pl.ds(pl.multiple_of(q * cw, 128), cw)], r4.at[o - 1], z_dev(o)))
    wait_all(cps)
    acc4[...] = acc3[:, pl.ds(pl.multiple_of(pz * cw, 128), cw)] + r4[0] + r4[1] + r4[2]

    row1 = pc * h1
    row2 = row1 + py * h2
    row3 = row2 + px * h3
    full[pl.ds(pl.multiple_of(row3, 8), h3), pl.ds(pl.multiple_of(pz * cw, 128), cw)] = acc4[...]

    mine = full.at[pl.ds(pl.multiple_of(row3, 8), h3), pl.ds(pl.multiple_of(pz * cw, 128), cw)]
    wait_all([send(mine, mine, z_dev(o)) for o in (1, 2, 3)])
    mine = full.at[pl.ds(pl.multiple_of(row3, 8), h3)]
    wait_all([send(mine, mine, x_dev(o)) for o in (1, 2, 3)])
    mine = full.at[pl.ds(pl.multiple_of(row2, 8), h2)]
    wait_all([send(mine, mine, y_dev(o)) for o in (1, 2, 3)])
    mine = full.at[pl.ds(pl.multiple_of(row1, 8), h1)]
    send(mine, mine, core_dev).wait()

    o_ref[...] = full[...]


def allreduce_all(x):
    rows, cols = x.shape
    h1 = rows // 2
    h2 = h1 // 4
    h3 = h2 // 4
    cw = cols // 4
    f32 = jnp.float32
    return pl.pallas_call(
        _allreduce_kernel,
        out_shape=jax.ShapeDtypeStruct((rows, cols), f32),
        in_specs=[pl.BlockSpec(memory_space=pltpu.VMEM)],
        out_specs=pl.BlockSpec(memory_space=pltpu.VMEM),
        scratch_shapes=[
            pltpu.VMEM((h1, cols), f32),
            pltpu.VMEM((h2, cols), f32),
            pltpu.VMEM((h3, cols), f32),
            pltpu.VMEM((h3, cw), f32),
            pltpu.VMEM((h1, cols), f32),
            pltpu.VMEM((3, h2, cols), f32),
            pltpu.VMEM((3, h3, cols), f32),
            pltpu.VMEM((3, h3, cw), f32),
            pltpu.VMEM((rows, cols), f32),
            pltpu.SemaphoreType.DMA((20,)),
            pltpu.SemaphoreType.DMA((20,)),
        ],
        compiler_params=pltpu.CompilerParams(collective_id=0, has_side_effects=True),
    )(x)


def _subspace_kernel(g_ref, b0_ref, o_ref):
    highest = lax.Precision.HIGHEST
    rank = b0_ref.shape[0]
    rows = lax.broadcasted_iota(jnp.int32, (rank, rank), 0)
    cols = lax.broadcasted_iota(jnp.int32, (rank, rank), 1)
    col_idx = lax.broadcasted_iota(jnp.int32, (rank, 1), 0)
    row_idx = lax.broadcasted_iota(jnp.int32, (1, rank), 1)
    eye = jnp.where(rows == cols, 1.0, 0.0).astype(jnp.float32)
    zero = jnp.zeros((rank, rank), jnp.float32)

    def cholesky_inverse(m):
        e = eye
        z = zero
        for j in range(rank):
            row_m = m[j:j + 1, :]
            col_m = m[:, j:j + 1]
            s = lax.rsqrt(m[j:j + 1, j:j + 1])
            c = jnp.where(col_idx >= j, col_m * s, 0.0)
            r = jnp.where(row_idx >= j, row_m * s, 0.0)
            m = m - c * r
            zr = e[j:j + 1, :] * s
            e = e - c * zr
            z = jnp.where(rows == j, zr, z)
        return z

    def sweep(_, basis_t):
        block_t = jnp.dot(basis_t, g_ref[...], precision=highest, preferred_element_type=jnp.float32)
        inner = lax.dot_general(block_t, block_t, (((1,), (1,)), ((), ())), precision=highest,
                                preferred_element_type=jnp.float32)
        l_inv = cholesky_inverse(inner)
        return jnp.dot(l_inv, block_t, precision=highest, preferred_element_type=jnp.float32)

    o_ref[...] = lax.fori_loop(0, ITERS, sweep, b0_ref[...])


def subspace_iterate(gram, start_basis):
    basis_t = pl.pallas_call(
        _subspace_kernel,
        out_shape=jax.ShapeDtypeStruct(start_basis.shape[::-1], jnp.float32),
        in_specs=[pl.BlockSpec(memory_space=pltpu.VMEM)] * 2,
        out_specs=pl.BlockSpec(memory_space=pltpu.VMEM),
    )(gram, start_basis.T)
    return basis_t.T


def _gram_kernel(s_hbm, o_ref, hi_hbm, lo_hbm, buf, hi_ref, lo_ref, cross_ref, sems, out_sems):
    _, cols, width = s_hbm.shape
    slots = buf.shape[0]
    groups = out_sems.shape[1]
    span = hi_ref.shape[1] // groups
    depth = span // width

    def copy(j):
        return pltpu.make_async_copy(s_hbm.at[:, j, :], buf.at[j % slots], sems.at[j % slots])

    def write_back(g):
        part = pl.ds(g * span, span)
        return (pltpu.make_async_copy(hi_ref.at[:, part], hi_hbm.at[:, part], out_sems.at[0, g]),
                pltpu.make_async_copy(lo_ref.at[:, part], lo_hbm.at[:, part], out_sems.at[1, g]))

    for j in range(slots - 1):
        copy(j).start()
    nt = (((1,), (1,)), ((), ()))
    for g in range(groups):
        for jj in range(depth):
            j = g * depth + jj
            if j + slots - 1 < cols:
                copy(j + slots - 1).start()
            copy(j).wait()
            x = buf[j % slots]
            hi = x.astype(jnp.bfloat16)
            lo = (x - hi.astype(jnp.float32)).astype(jnp.bfloat16)
            hi_ref[:, j * width:(j + 1) * width] = hi
            lo_ref[:, j * width:(j + 1) * width] = lo
        for cp in write_back(g):
            cp.start()
        part = pl.ds(g * span, span)
        hh = lax.dot_general(hi_ref[:, part], hi_ref[:, part], nt, preferred_element_type=jnp.float32)
        hl = lax.dot_general(hi_ref[:, part], lo_ref[:, part], nt, preferred_element_type=jnp.float32)
        if g == 0:
            o_ref[...] = hh
            cross_ref[...] = hl
        else:
            o_ref[...] += hh
            cross_ref[...] += hl
    o_ref[...] += cross_ref[...] + cross_ref[...].T
    for g in range(groups):
        for cp in write_back(g):
            cp.wait()


def local_gram(slab, depth=16, slots=16):
    rows, cols, width = slab.shape
    groups = cols // depth
    flat = jax.ShapeDtypeStruct((rows, cols * width), jnp.bfloat16)
    return pl.pallas_call(
        _gram_kernel,
        out_shape=(jax.ShapeDtypeStruct((rows, rows), jnp.float32), flat, flat),
        in_specs=[pl.BlockSpec(memory_space=pl.ANY)],
        out_specs=(pl.BlockSpec(memory_space=pltpu.VMEM), pl.BlockSpec(memory_space=pl.ANY),
                   pl.BlockSpec(memory_space=pl.ANY)),
        scratch_shapes=[
            pltpu.VMEM((slots, rows, width), jnp.float32),
            pltpu.VMEM((rows, cols * width), jnp.bfloat16),
            pltpu.VMEM((rows, cols * width), jnp.bfloat16),
            pltpu.VMEM((rows, rows), jnp.float32),
            pltpu.SemaphoreType.DMA((slots,)),
            pltpu.SemaphoreType.DMA((2, groups)),
        ],
        compiler_params=pltpu.CompilerParams(vmem_limit_bytes=56 * 1024 * 1024),
    )(slab)

def _project_kernel(b_ref, xh_ref, xl_ref, o_ref):
    f32 = jnp.float32
    b = b_ref[...]
    bh = b.astype(jnp.bfloat16)
    bl = (b - bh.astype(f32)).astype(jnp.bfloat16)
    xh = xh_ref[...]
    res = (jnp.dot(bh, xh, preferred_element_type=f32) + jnp.dot(bh, xl_ref[...], preferred_element_type=f32)
           + jnp.dot(bl, xh, preferred_element_type=f32))
    width = o_ref.shape[2]
    for jj in range(o_ref.shape[1]):
        o_ref[:, jj, :] = res[:, jj * width:(jj + 1) * width]


def project(basis_t, x_hi, x_lo, cols, depth, tile=2048):
    rank, rows = basis_t.shape
    width = x_hi.shape[1]
    per = tile // depth
    return pl.pallas_call(
        _project_kernel,
        out_shape=jax.ShapeDtypeStruct((rank, cols, depth), jnp.float32),
        grid=(width // tile,),
        in_specs=[pl.BlockSpec((rank, rows), lambda g: (0, 0)),
                  pl.BlockSpec((rows, tile), lambda g: (0, g)), pl.BlockSpec((rows, tile), lambda g: (0, g))],
        out_specs=pl.BlockSpec((rank, per, depth), lambda g: (0, g, 0)),
    )(basis_t, x_hi, x_lo)


def shards(wide, tensor_slab, start_basis):
    highest = lax.Precision.HIGHEST
    high = lax.Precision.HIGH
    _, cols, depth = tensor_slab.shape
    basis = start_basis
    gram_part, slab_hi, slab_lo = local_gram(tensor_slab)
    gram_full = allreduce_all(gram_part)
    basis = subspace_iterate(gram_full, start_basis)
    proj = project(basis.T, slab_hi, slab_lo, cols, depth)
    proj = lax.all_to_all(proj, "wide", split_axis=0, concat_axis=1, tiled=True)
    core_unfold = jnp.transpose(proj, (2, 0, 1))
    return (basis, core_unfold)


def solution(mesh):
    placed = (P(None, "wide", "narrow"), P())
    return jax.shard_map(
        functools.partial(shards, mesh.shape["wide"]),
        mesh=mesh,
        in_specs=placed,
        out_specs=(P(), P("narrow", "wide", None)),
        check_vma=False,
    )
```

```python
import functools

import jax
import jax.numpy as jnp
from jax import lax
from jax.experimental import pallas as pl
from jax.experimental.pallas import tpu as pltpu
from jax.sharding import PartitionSpec as P

I1 = 512
ITERS = 8
MESH = pl.DeviceIdType.MESH


def orthonormal(block, inner):
    lower_factor = jnp.linalg.cholesky(inner)
    return jax.scipy.linalg.solve_triangular(lower_factor, block.T, lower=True).T


def _allreduce_kernel(x_ref, o_ref, acc1, acc2, acc3, acc4, r1, r2, r3, r4, full, send_sems, recv_sems):
    w = lax.axis_index("wide")
    n = lax.axis_index("narrow")
    px, pz = w // 4, w % 4
    py, pc = n // 2, n % 2
    rows, cols = x_ref.shape
    h1 = rows // 2
    h2 = h1 // 4
    h3 = h2 // 4
    cw = cols // 4

    core_dev = (w, py * 2 + (1 - pc))

    def y_dev(o):
        return (w, ((py + o) % 4) * 2 + pc)

    def x_dev(o):
        return (((px + o) % 4) * 4 + pz, n)

    def z_dev(o):
        return (px * 4 + (pz + o) % 4, n)

    partners = [core_dev] + [y_dev(o) for o in (1, 2, 3)] + [x_dev(o) for o in (1, 2, 3)] + [z_dev(o) for o in (1, 2, 3)]
    barrier = pltpu.get_barrier_semaphore()
    for dev in partners:
        pl.semaphore_signal(barrier, inc=1, device_id=dev, device_id_type=MESH)
    pl.semaphore_wait(barrier, len(partners))

    slot = [0]

    def send(src, dst, dev):
        k = slot[0]
        slot[0] += 1
        cp = pltpu.make_async_remote_copy(
            src_ref=src, dst_ref=dst, send_sem=send_sems.at[k], recv_sem=recv_sems.at[k],
            device_id=dev, device_id_type=MESH)
        cp.start()
        return cp

    def wait_all(cps):
        for cp in cps:
            cp.wait()

    cp = send(x_ref.at[pl.ds(pl.multiple_of((1 - pc) * h1, 8), h1)], r1, core_dev)
    cp.wait()
    acc1[...] = x_ref[pl.ds(pl.multiple_of(pc * h1, 8), h1), :] + r1[...]

    cps = []
    for o in (1, 2, 3):
        q = (py + o) % 4
        cps.append(send(acc1.at[pl.ds(pl.multiple_of(q * h2, 8), h2)], r2.at[o - 1], y_dev(o)))
    wait_all(cps)
    acc2[...] = acc1[pl.ds(pl.multiple_of(py * h2, 8), h2), :] + r2[0] + r2[1] + r2[2]

    cps = []
    for o in (1, 2, 3):
        q = (px + o) % 4
        cps.append(send(acc2.at[pl.ds(pl.multiple_of(q * h3, 8), h3)], r3.at[o - 1], x_dev(o)))
    wait_all(cps)
    acc3[...] = acc2[pl.ds(pl.multiple_of(px * h3, 8), h3), :] + r3[0] + r3[1] + r3[2]

    cps = []
    for o in (1, 2, 3):
        q = (pz + o) % 4
        cps.append(send(acc3.at[:, pl.ds(pl.multiple_of(q * cw, 128), cw)], r4.at[o - 1], z_dev(o)))
    wait_all(cps)
    acc4[...] = acc3[:, pl.ds(pl.multiple_of(pz * cw, 128), cw)] + r4[0] + r4[1] + r4[2]

    row1 = pc * h1
    row2 = row1 + py * h2
    row3 = row2 + px * h3
    full[pl.ds(pl.multiple_of(row3, 8), h3), pl.ds(pl.multiple_of(pz * cw, 128), cw)] = acc4[...]

    mine = full.at[pl.ds(pl.multiple_of(row3, 8), h3), pl.ds(pl.multiple_of(pz * cw, 128), cw)]
    wait_all([send(mine, mine, z_dev(o)) for o in (1, 2, 3)])
    mine = full.at[pl.ds(pl.multiple_of(row3, 8), h3)]
    wait_all([send(mine, mine, x_dev(o)) for o in (1, 2, 3)])
    mine = full.at[pl.ds(pl.multiple_of(row2, 8), h2)]
    wait_all([send(mine, mine, y_dev(o)) for o in (1, 2, 3)])
    mine = full.at[pl.ds(pl.multiple_of(row1, 8), h1)]
    send(mine, mine, core_dev).wait()

    o_ref[...] = full[...]


def allreduce_all(x):
    rows, cols = x.shape
    h1 = rows // 2
    h2 = h1 // 4
    h3 = h2 // 4
    cw = cols // 4
    f32 = jnp.float32
    return pl.pallas_call(
        _allreduce_kernel,
        out_shape=jax.ShapeDtypeStruct((rows, cols), f32),
        in_specs=[pl.BlockSpec(memory_space=pltpu.VMEM)],
        out_specs=pl.BlockSpec(memory_space=pltpu.VMEM),
        scratch_shapes=[
            pltpu.VMEM((h1, cols), f32),
            pltpu.VMEM((h2, cols), f32),
            pltpu.VMEM((h3, cols), f32),
            pltpu.VMEM((h3, cw), f32),
            pltpu.VMEM((h1, cols), f32),
            pltpu.VMEM((3, h2, cols), f32),
            pltpu.VMEM((3, h3, cols), f32),
            pltpu.VMEM((3, h3, cw), f32),
            pltpu.VMEM((rows, cols), f32),
            pltpu.SemaphoreType.DMA((20,)),
            pltpu.SemaphoreType.DMA((20,)),
        ],
        compiler_params=pltpu.CompilerParams(collective_id=0, has_side_effects=True),
    )(x)


def _subspace_kernel(g_ref, b0_ref, o_ref):
    highest = lax.Precision.HIGHEST
    rank = b0_ref.shape[0]
    rows = lax.broadcasted_iota(jnp.int32, (rank, rank), 0)
    cols = lax.broadcasted_iota(jnp.int32, (rank, rank), 1)
    col_idx = lax.broadcasted_iota(jnp.int32, (rank, 1), 0)
    row_idx = lax.broadcasted_iota(jnp.int32, (1, rank), 1)
    eye = jnp.where(rows == cols, 1.0, 0.0).astype(jnp.float32)
    zero = jnp.zeros((rank, rank), jnp.float32)

    def cholesky_inverse(m):
        e = eye
        z = zero
        for j in range(rank):
            row_m = m[j:j + 1, :]
            col_m = m[:, j:j + 1]
            s = lax.rsqrt(m[j:j + 1, j:j + 1])
            c = jnp.where(col_idx >= j, col_m * s, 0.0)
            r = jnp.where(row_idx >= j, row_m * s, 0.0)
            m = m - c * r
            zr = e[j:j + 1, :] * s
            e = e - c * zr
            z = jnp.where(rows == j, zr, z)
        return z

    def sweep(_, basis_t):
        block_t = jnp.dot(basis_t, g_ref[...], precision=highest, preferred_element_type=jnp.float32)
        inner = lax.dot_general(block_t, block_t, (((1,), (1,)), ((), ())), precision=highest,
                                preferred_element_type=jnp.float32)
        l_inv = cholesky_inverse(inner)
        return jnp.dot(l_inv, block_t, precision=highest, preferred_element_type=jnp.float32)

    o_ref[...] = lax.fori_loop(0, ITERS, sweep, b0_ref[...])


def subspace_iterate(gram, start_basis):
    basis_t = pl.pallas_call(
        _subspace_kernel,
        out_shape=jax.ShapeDtypeStruct(start_basis.shape[::-1], jnp.float32),
        in_specs=[pl.BlockSpec(memory_space=pltpu.VMEM)] * 2,
        out_specs=pl.BlockSpec(memory_space=pltpu.VMEM),
    )(gram, start_basis.T)
    return basis_t.T


def _gram_kernel(s_hbm, o_ref, hi_hbm, lo_hbm, buf, hi_ref, lo_ref, cross_ref, sems, out_sems):
    _, cols, width = s_hbm.shape
    slots = buf.shape[0]
    groups = out_sems.shape[1]
    span = hi_ref.shape[1] // groups
    depth = span // width

    def copy(j):
        return pltpu.make_async_copy(s_hbm.at[:, j, :], buf.at[j % slots], sems.at[j % slots])

    def write_back(g):
        part = pl.ds(g * span, span)
        return (pltpu.make_async_copy(hi_ref.at[:, part], hi_hbm.at[:, part], out_sems.at[0, g]),
                pltpu.make_async_copy(lo_ref.at[:, part], lo_hbm.at[:, part], out_sems.at[1, g]))

    for j in range(slots - 1):
        copy(j).start()
    nt = (((1,), (1,)), ((), ()))
    for g in range(groups):
        for jj in range(depth):
            j = g * depth + jj
            if j + slots - 1 < cols:
                copy(j + slots - 1).start()
            copy(j).wait()
            x = buf[j % slots]
            hi = x.astype(jnp.bfloat16)
            lo = (x - hi.astype(jnp.float32)).astype(jnp.bfloat16)
            hi_ref[:, j * width:(j + 1) * width] = hi
            lo_ref[:, j * width:(j + 1) * width] = lo
        for cp in write_back(g):
            cp.start()
        part = pl.ds(g * span, span)
        hh = lax.dot_general(hi_ref[:, part], hi_ref[:, part], nt, preferred_element_type=jnp.float32)
        hl = lax.dot_general(hi_ref[:, part], lo_ref[:, part], nt, preferred_element_type=jnp.float32)
        if g == 0:
            o_ref[...] = hh
            cross_ref[...] = hl
        else:
            o_ref[...] += hh
            cross_ref[...] += hl
    o_ref[...] += cross_ref[...] + cross_ref[...].T
    for g in range(groups):
        for cp in write_back(g):
            cp.wait()


def local_gram(slab, depth=8, slots=32):
    rows, cols, width = slab.shape
    groups = cols // depth
    flat = jax.ShapeDtypeStruct((rows, cols * width), jnp.bfloat16)
    return pl.pallas_call(
        _gram_kernel,
        out_shape=(jax.ShapeDtypeStruct((rows, rows), jnp.float32), flat, flat),
        in_specs=[pl.BlockSpec(memory_space=pl.ANY)],
        out_specs=(pl.BlockSpec(memory_space=pltpu.VMEM), pl.BlockSpec(memory_space=pl.ANY),
                   pl.BlockSpec(memory_space=pl.ANY)),
        scratch_shapes=[
            pltpu.VMEM((slots, rows, width), jnp.float32),
            pltpu.VMEM((rows, cols * width), jnp.bfloat16),
            pltpu.VMEM((rows, cols * width), jnp.bfloat16),
            pltpu.VMEM((rows, rows), jnp.float32),
            pltpu.SemaphoreType.DMA((slots,)),
            pltpu.SemaphoreType.DMA((2, groups)),
        ],
        compiler_params=pltpu.CompilerParams(vmem_limit_bytes=56 * 1024 * 1024),
    )(slab)

def _project_kernel(b_ref, xh_ref, xl_ref, o_ref):
    f32 = jnp.float32
    b = b_ref[...]
    bh = b.astype(jnp.bfloat16)
    bl = (b - bh.astype(f32)).astype(jnp.bfloat16)
    xh = xh_ref[...]
    res = (jnp.dot(bh, xh, preferred_element_type=f32) + jnp.dot(bh, xl_ref[...], preferred_element_type=f32)
           + jnp.dot(bl, xh, preferred_element_type=f32))
    width = o_ref.shape[2]
    for jj in range(o_ref.shape[1]):
        o_ref[:, jj, :] = res[:, jj * width:(jj + 1) * width]


def project(basis_t, x_hi, x_lo, cols, depth, tile=2048):
    rank, rows = basis_t.shape
    width = x_hi.shape[1]
    per = tile // depth
    return pl.pallas_call(
        _project_kernel,
        out_shape=jax.ShapeDtypeStruct((rank, cols, depth), jnp.float32),
        grid=(width // tile,),
        in_specs=[pl.BlockSpec((rank, rows), lambda g: (0, 0)),
                  pl.BlockSpec((rows, tile), lambda g: (0, g)), pl.BlockSpec((rows, tile), lambda g: (0, g))],
        out_specs=pl.BlockSpec((rank, per, depth), lambda g: (0, g, 0)),
    )(basis_t, x_hi, x_lo)


def shards(wide, tensor_slab, start_basis):
    highest = lax.Precision.HIGHEST
    high = lax.Precision.HIGH
    _, cols, depth = tensor_slab.shape
    basis = start_basis
    gram_part, slab_hi, slab_lo = local_gram(tensor_slab)
    gram_full = allreduce_all(gram_part)
    basis = subspace_iterate(gram_full, start_basis)
    proj = project(basis.T, slab_hi, slab_lo, cols, depth)
    proj = lax.all_to_all(proj, "wide", split_axis=0, concat_axis=1, tiled=True)
    core_unfold = jnp.transpose(proj, (2, 0, 1))
    return (basis, core_unfold)


def solution(mesh):
    placed = (P(None, "wide", "narrow"), P())
    return jax.shard_map(
        functools.partial(shards, mesh.shape["wide"]),
        mesh=mesh,
        in_specs=placed,
        out_specs=(P(), P("narrow", "wide", None)),
        check_vma=False,
    )
```
